32 devices in a mesh: seqs: 2 (over x), ctx: 16 (over z, y, core).
Axes of the slice: x: 2, y: 2, z: 4, core: 2. Of those that a mesh axis runs over, the one named last changes fastest.
Arguments:
- queries: bfloat16 [16384, 2048], P(('seqs', 'ctx')), parts along dimension 0, may hold values from -5 to 5
- keys: bfloat16 [16384, 2048], P(('seqs', 'ctx')), parts along dimension 0, may hold values from -5 to 5
- values: bfloat16 [16384, 2048], P(('seqs', 'ctx')), parts along dimension 0, may hold values from -6 to 6
- x_in: bfloat16 [16384, 2048], P(('seqs', 'ctx')), parts along dimension 0, may hold values from -6 to 6
- log_decay: float32 [16384, 32], P(('seqs', 'ctx')), parts along dimension 0, may hold values from -0.7 to 0, as said below
- b_in: bfloat16 [16384, 64], P(('seqs', 'ctx')), parts along dimension 0, may hold values from -0.75 to 0.75
- c_in: bfloat16 [16384, 64], P(('seqs', 'ctx')), parts along dimension 0, may hold values from -0.125 to 0.125
- skip_d: float32 [32], replicated, may hold values from 0.5 to 2
Outputs:
- attended: bfloat16 [16384, 2048], P(('seqs', 'ctx')), parts along dimension 0
- scan_out: bfloat16 [16384, 2048], P(('seqs', 'ctx')), parts along dimension 0
The draws below stay inside these ranges and needn't reach their ends.
There are 2 independent parts, one for each index of `seqs`. The reference program is written for one: setup_inputs(seed, part) draws one part's arguments, and reference() takes and returns one part's arrays. A program takes and returns all parts, laid end to end along the dimension named above; an argument that names none is the same for every part. Nothing has to cross between parts.
Inputs may be any that keep to these rules, and one draw needn't show every extreme that they name: log_decay is negative in every entry.
All inputs are finite; a program needn't handle non-finite values.
Results may differ from the reference program's by a relative error of at most 0.0043.
Values may be sent and summed in bfloat16 or wider, within the bound.
No kernel may reach another device: no remote copies, remote signals or barrier semaphores. Data moves between devices by JAX's collectives and lax.ppermute only.
A program may use at most 384 MiB of HBM per device.

```python
import math
import jax
import jax.numpy as jnp
from jax import lax

TOK_DEV = 512
WINDOW = 2048
AH = 16
HD = 128
SCAN_HEADS = 32
P_SIZE = 64
N = 64
TOKEN_COUNT = 8192


def attention_draws(key):
    base = jax.random.fold_in(key, 7919)
    parallel_flows = jax.random.split(base, 2)
    shape = (TOKEN_COUNT, AH * HD)
    query_rows = jnp.clip(jax.random.normal(parallel_flows[0], shape, jnp.float32), -5.0, 5.0)
    key_rows = jnp.clip(jax.random.normal(parallel_flows[1], shape, jnp.float32), -5.0, 5.0)
    return (query_rows, key_rows)


def draw_queries(key, part):
    return attention_draws(key)[0].astype(jnp.bfloat16)


def draw_keys(key, part):
    return attention_draws(key)[1].astype(jnp.bfloat16)


def draw_log_decay(key, part):
    base = jax.random.fold_in(key, 3571)
    parallel_flows = jax.random.split(base, 6)
    slow_share = 0.5
    gradual_heads = jax.random.bernoulli(parallel_flows[0], slow_share, (SCAN_HEADS,))
    slow_total = jnp.exp(jax.random.uniform(parallel_flows[1], (SCAN_HEADS,), jnp.float32, math.log(0.1), math.log(0.5)))
    fast_rate = jnp.exp(jax.random.uniform(parallel_flows[2], (SCAN_HEADS,), jnp.float32, math.log(0.02), math.log(0.035)))
    step_frequency = jnp.where(gradual_heads, slow_total / TOKEN_COUNT, fast_rate)
    jitter_level = jax.random.uniform(parallel_flows[3], (TOKEN_COUNT, SCAN_HEADS), jnp.float32, 0.5, 1.5)
    spike_locations = jax.random.randint(parallel_flows[4], (2,), 0, TOKEN_COUNT)
    token_position = jnp.arange(TOKEN_COUNT, dtype=jnp.int32)
    spike_row = jnp.any(token_position[:, None] == spike_locations[None, :], axis=1)
    spike_length = jax.random.uniform(parallel_flows[5], (TOKEN_COUNT, SCAN_HEADS), jnp.float32, 0.2, 0.45)
    spike_event = jnp.where(spike_row[:, None] & gradual_heads[None, :], -jnp.log(1.0 - spike_length), 0.0)
    return -(step_frequency[None, :] * jitter_level) - spike_event


def level_of(own_key, dims, shards, low, top_value):
    def one(position, blocks):
        steps = jax.random.uniform(jax.random.fold_in(jax.random.fold_in(own_key, 6), position), (blocks,), jnp.float32, low / len(shards), top_value / len(shards))
        return jnp.repeat(jnp.exp(steps), dims[position] // blocks).reshape((-1,) + (1,) * (len(dims) - position - 1))

    level = one(*shards[0])
    for cut in shards[1:]:
        level = level * one(*cut)
    return level


def bell_draw(own_key, dims, spread, bound, cuts=(), kind=jnp.bfloat16):
    values = jax.random.normal(own_key, dims, jnp.float32) * spread
    if len(cuts) > 0:
        values = level_of(own_key, dims, cuts, -0.22, 0.18) * values
    return jnp.clip(values, min=-bound, max=bound).astype(kind)


def setup_inputs(seed: int = 0, part: int = 0) -> dict:
    key_of = jax.random.split(jax.random.key(seed), 9)
    part_splits = jax.random.split(jax.random.fold_in(key_of[8], part), 9)
    return {
        "queries": draw_queries(jax.random.fold_in(jax.random.fold_in(key_of[8], part), 71), part),
        "keys": draw_keys(jax.random.fold_in(jax.random.fold_in(key_of[8], part), 71), part),
        "values": bell_draw(part_splits[2], (TOKEN_COUNT, AH * HD), 1.0, 6.0, ((0, 16),)),
        "x_in": bell_draw(part_splits[3], (TOKEN_COUNT, SCAN_HEADS * P_SIZE), 1.0, 6.0, ((0, 16),)),
        "log_decay": draw_log_decay(jax.random.fold_in(jax.random.fold_in(key_of[8], part), 71), part),
        "b_in": bell_draw(part_splits[5], (TOKEN_COUNT, N), N ** -0.5, 0.75, ((0, 16),)),
        "c_in": bell_draw(part_splits[6], (TOKEN_COUNT, N), (4 * TOK_DEV) ** -0.5, 0.125, ((0, 16),)),
        "skip_d": jnp.clip(jnp.exp(jax.random.uniform(key_of[7], (SCAN_HEADS,), jnp.float32, math.log(0.5), math.log(2.0))), 0.5, 2.0),
    }


def attend_all(queries, keys, values):
    padding = jnp.zeros((WINDOW, AH * HD), queries.dtype)
    keys_padded = jnp.concatenate([padding, keys], axis=0)
    values_padded = jnp.concatenate([padding, values], axis=0)

    def one_block(index):
        start = (index * TOK_DEV).astype(jnp.int32)
        query_rows = lax.dynamic_slice_in_dim(queries, start, TOK_DEV, 0)
        key_rows = lax.dynamic_slice_in_dim(keys_padded, start, TOK_DEV + WINDOW, 0)
        value_rows = lax.dynamic_slice_in_dim(values_padded, start, TOK_DEV + WINDOW, 0)
        query_pos = start + jnp.arange(TOK_DEV, dtype=jnp.int32)
        key_pos = start - WINDOW + jnp.arange(TOK_DEV + WINDOW, dtype=jnp.int32)
        allowed = (key_pos[None, :] <= query_pos[:, None]) & (key_pos[None, :] > query_pos[:, None] - WINDOW) & (key_pos[None, :] >= 0)
        query_heads = query_rows.reshape(TOK_DEV, AH, HD).astype(jnp.float32)
        key_heads = key_rows.reshape(TOK_DEV + WINDOW, AH, HD).astype(jnp.float32)
        value_heads = value_rows.reshape(TOK_DEV + WINDOW, AH, HD).astype(jnp.float32)
        scores = jnp.einsum("ihd,jhd->hij", query_heads, key_heads) * (HD ** -0.5)
        scores = jnp.where(allowed[None], scores, -1e30)
        row_max = jnp.max(scores, axis=2, keepdims=True)
        probs = jnp.where(allowed[None], jnp.exp(scores - row_max), 0.0)
        totals = jnp.sum(probs, axis=2)
        weights = probs.astype(jnp.bfloat16).astype(jnp.float32)
        summed = jnp.einsum("hij,jhd->ihd", weights, value_heads)
        result = summed / jnp.transpose(totals)[:, :, None]
        return result.astype(jnp.bfloat16).reshape(TOK_DEV, AH * HD)

    blocks = lax.map(one_block, jnp.arange(TOKEN_COUNT // TOK_DEV, dtype=jnp.int32))
    return blocks.reshape(TOKEN_COUNT, AH * HD)


def scan_all(x_in, log_decay, b_in, c_in, skip_d):
    count = TOKEN_COUNT // TOK_DEV
    x_blocks = x_in.reshape(count, TOK_DEV, SCAN_HEADS, P_SIZE)
    decay_blocks = log_decay.reshape(count, TOK_DEV, SCAN_HEADS)
    b_blocks = b_in.reshape(count, TOK_DEV, N)
    c_blocks = c_in.reshape(count, TOK_DEV, N)
    order_mask = jnp.arange(TOK_DEV)[:, None] >= jnp.arange(TOK_DEV)[None, :]

    def step_block(carried, block):
        x_block, decay_block, b_block, c_block = block
        cumulative = jnp.cumsum(decay_block, axis=0)
        block_total = cumulative[-1]
        gaps = jnp.transpose(cumulative)[:, :, None] - jnp.transpose(cumulative)[:, None, :]
        decay_mat = jnp.where(order_mask[None], jnp.exp(jnp.where(order_mask[None], gaps, 0.0)), 0.0)
        intersections = jnp.dot(c_block, jnp.transpose(b_block), preferred_element_type=jnp.float32)
        mixing = (decay_mat * intersections[None]).astype(jnp.bfloat16)
        x_float = x_block.astype(jnp.float32)
        within = jnp.einsum("htu,uhp->thp", mixing.astype(jnp.float32), x_float)
        weighted = (x_float * jnp.exp(block_total[None, :] - cumulative)[:, :, None]).astype(jnp.bfloat16)
        own_state = jnp.einsum("thp,tn->hpn", weighted.astype(jnp.float32), b_block.astype(jnp.float32))
        inter = jnp.exp(cumulative)[:, :, None] * jnp.einsum("tn,hpn->thp", c_block.astype(jnp.float32), carried, precision=lax.Precision.HIGHEST)
        result = within + inter + skip_d[None, :, None] * x_float
        carried_next = jnp.exp(block_total)[:, None, None] * carried + own_state
        return carried_next, result.astype(jnp.bfloat16).reshape(TOK_DEV, SCAN_HEADS * P_SIZE)

    start_state = jnp.zeros((SCAN_HEADS, P_SIZE, N), jnp.float32)
    final_state, outputs = lax.scan(step_block, start_state, (x_blocks, decay_blocks, b_blocks, c_blocks))
    return outputs.reshape(TOKEN_COUNT, SCAN_HEADS * P_SIZE)


def reference(queries, keys, values, x_in, log_decay, b_in, c_in, skip_d):
    attended = attend_all(queries, keys, values)
    scan_out = scan_all(x_in, log_decay, b_in, c_in, skip_d)
    return (attended, scan_out)
```

```python
import functools

import jax
import jax.numpy as jnp
from jax import lax
from jax.experimental import pallas as pl
from jax.experimental.pallas import tpu as pltpu
from jax.sharding import PartitionSpec as P

TOK_DEV = 512
WINDOW = 2048
AH = 16
HD = 128
SCAN_HEADS = 32
P_SIZE = 64
N = 64
GROUP = WINDOW // TOK_DEV
SUB = 128
CHUNKS = (2, 2, 2, 2, 2, 2, 2, 2)
NEG = -1e30
EXP_SCALE = HD ** (-0.5) * 1.4426950408889634
F32 = jnp.float32
BF16 = jnp.bfloat16


def cyclic(array, by):
    count = lax.axis_size("ctx")
    return lax.ppermute(array, "ctx", [(i, (i + by) % count) for i in range(count)])


def swapped(array, bit):
    count = lax.axis_size("ctx")
    return lax.ppermute(array, "ctx", [(i, i ^ bit) for i in range(count)])


def dot_t(a, b):
    return lax.dot_general(a, b, (((1,), (1,)), ((), ())), preferred_element_type=F32)


def dot_f32(a, b):
    return jnp.dot(a, b, preferred_element_type=F32)


def attend_kernel(flags, q, k, v, z, d, e, g, xk, xv, out, keys, vals):
    odd = flags[0]
    later = flags[1]
    full = flags[2]

    @pl.when(pl.program_id(0) == 0)
    def _():
        vals[:, :, HD:] = jnp.ones((5, TOK_DEV, HD), BF16)

    keys[0] = k[...]
    vals[0, :, :HD] = v[...]
    keys[1] = z[0]
    vals[1, :, :HD] = z[1]
    keys[2] = d[0]
    vals[2, :, :HD] = d[1]

    @pl.when(odd == 1)
    def _():
        keys[3] = xk[...]
        vals[3, :, :HD] = xv[...]

    @pl.when(odd == 0)
    def _():
        keys[3] = e[0]
        vals[3, :, :HD] = e[1]

    keys[4] = g[0]
    vals[4, :, :HD] = g[1]

    def tile(first, rows, masked):
        qt = q[first : first + rows, :]
        row = lax.broadcasted_iota(jnp.int32, (rows, TOK_DEV), 0) + first
        col = lax.broadcasted_iota(jnp.int32, (rows, TOK_DEV), 1)
        causal = col <= row
        own = dot_t(qt, keys[0])
        prev = dot_t(qt, keys[1])
        s2 = dot_t(qt, keys[2])
        s3 = dot_t(qt, keys[3])
        s4 = dot_t(qt, keys[4])
        if masked:
            prev = jnp.full_like(prev, NEG)
            bias_d = jnp.where(later == 1, 0.0, NEG)
            bias_e = jnp.where(odd == 1, 0.0, NEG)
            s2 = s2 + bias_d
            s3 = s3 + bias_e
            s4 = s4 + bias_d
        s0 = jnp.where(causal, own, prev)
        top = jnp.maximum(jnp.maximum(s0, s2), jnp.maximum(s3, s4))
        top = jnp.max(top, axis=1, keepdims=True) * EXP_SCALE
        p0 = jnp.exp2(s0 * EXP_SCALE - top)
        p2 = jnp.exp2(s2 * EXP_SCALE - top).astype(BF16)
        p3 = jnp.exp2(s3 * EXP_SCALE - top).astype(BF16)
        p4 = jnp.exp2(s4 * EXP_SCALE - top).astype(BF16)
        po = jnp.where(causal, p0, 0.0).astype(BF16)
        pp = jnp.where(causal, 0.0, p0).astype(BF16)
        acc = dot_f32(po, vals[0]) + dot_f32(pp, vals[1])
        acc = acc + dot_f32(p2, vals[2]) + dot_f32(p3, vals[3]) + dot_f32(p4, vals[4])
        out[first : first + rows, :] = (acc[:, :HD] / acc[:, HD:]).astype(BF16)

    @pl.when(full == 1)
    def _():
        for first in range(0, TOK_DEV, 128):
            tile(first, 128, False)

    @pl.when(full == 0)
    def _():
        for first in range(0, TOK_DEV, 128):
            tile(first, 128, True)


def attend(flags, low, heads, queries, keys, values, z, d, e, g, xk, xv):
    wide = pl.BlockSpec((TOK_DEV, HD), lambda j, f: (0, low + j))
    pair = pl.BlockSpec((2, TOK_DEV, HD), lambda j, f: (0, 0, j))
    return pl.pallas_call(
        attend_kernel,
        name="attend",
        out_shape=jax.ShapeDtypeStruct((TOK_DEV, heads * HD), BF16),
        grid_spec=pltpu.PrefetchScalarGridSpec(
            num_scalar_prefetch=1,
            grid=(heads,),
            in_specs=[wide, wide, wide, pair, pair, pair, pair, wide, wide],
            out_specs=pl.BlockSpec((TOK_DEV, HD), lambda j, f: (0, j)),
            scratch_shapes=[
                pltpu.VMEM((5, TOK_DEV, HD), BF16),
                pltpu.VMEM((5, TOK_DEV, 2 * HD), BF16),
            ],
        ),
        compiler_params=pltpu.CompilerParams(vmem_limit_bytes=32 << 20),
    )(flags, queries, keys, values, z, d, e, g, xk, xv)


def split3(a):
    hi = a.astype(BF16)
    rest = a - hi.astype(F32)
    mid = rest.astype(BF16)
    low = (rest - mid.astype(F32)).astype(BF16)
    return hi, mid, low


def split2(a):
    hi = a.astype(BF16)
    return hi, (a - hi.astype(F32)).astype(BF16)


def pick(head, width):
    row = lax.broadcasted_iota(jnp.int32, (3 * SCAN_HEADS, width), 0) % SCAN_HEADS
    return (row == head).astype(BF16)


def local_kernel(x, decay, decay_t, b, c, skip, part, state, cum_out, cums, cum_t, cross):
    step = pl.program_id(0)

    @pl.when(step == 0)
    def _():
        t = lax.broadcasted_iota(jnp.int32, (TOK_DEV, TOK_DEV), 0)
        u = lax.broadcasted_iota(jnp.int32, (TOK_DEV, TOK_DEV), 1)
        lower = (t >= u).astype(BF16)
        upper = (t <= u).astype(BF16)
        hi, mid, low = split3(decay[...])
        total = dot_f32(lower, hi) + dot_f32(lower, mid) + dot_f32(lower, low)
        cum_out[...] = total
        hi, mid, low = split3(total)
        cums[:, 0:32] = hi
        cums[:, 32:64] = mid
        cums[:, 64:96] = low
        hi, mid, low = split3(decay_t[...])
        cum_t[...] = dot_f32(hi, upper) + dot_f32(mid, upper) + dot_f32(low, upper)
        for s in range(TOK_DEV // SUB):
            at = pl.ds(s * SUB, SUB)
            cross[at, :] = dot_t(c[at, :], b[at, :])

    t = lax.broadcasted_iota(jnp.int32, (SUB, SUB), 0)
    u = lax.broadcasted_iota(jnp.int32, (SUB, SUB), 1)
    lower = t >= u
    left = u < P_SIZE
    first = 2 * step
    cum_a = dot_f32(cums[...], pick(first, SUB))
    cum_b = dot_f32(cums[...], pick(first + 1, SUB))
    row_a = cum_t[pl.ds(first, 1), :]
    row_b = cum_t[pl.ds(first + 1, 1), :]
    carry = jnp.zeros((N, SUB), F32)
    before = jnp.zeros((1, SUB), F32)
    for s in range(TOK_DEV // SUB):
        at = pl.ds(s * SUB, SUB)
        a = cum_a[s * SUB : (s + 1) * SUB, :]
        bb = cum_b[s * SUB : (s + 1) * SUB, :]
        both = jnp.where(left, a, bb)
        xs = x[at, :]
        xf = xs.astype(F32)
        inner = cross[at, :]
        gap_a = jnp.where(lower, a - row_a[:, s * SUB : (s + 1) * SUB], NEG)
        gap_b = jnp.where(lower, bb - row_b[:, s * SUB : (s + 1) * SUB], NEG)
        mix_a = (jnp.exp(gap_a) * inner).astype(BF16)
        mix_b = (jnp.exp(gap_b) * inner).astype(BF16)
        x_a = jnp.where(left, xf, 0.0).astype(BF16)
        x_b = jnp.where(left, 0.0, xf).astype(BF16)
        y = dot_f32(
            jnp.concatenate([mix_a, mix_b], axis=1), jnp.concatenate([x_a, x_b], axis=0)
        )
        if s > 0:
            hi, low = split2(carry)
            cs = c[at, :]
            reach = dot_f32(
                jnp.concatenate([cs, cs], axis=1), jnp.concatenate([hi, low], axis=0)
            )
            y = y + jnp.exp(both - before) * reach
        part[at, :] = y + skip[...] * xf
        end = both[SUB - 1 : SUB, :]
        weighted = (xf * jnp.exp(end - both)).astype(BF16)
        added = lax.dot_general(
            b[at, :], weighted, (((0,), (0,)), ((), ())), preferred_element_type=F32
        )
        carry = jnp.exp(end - before) * carry + added
        before = end
    state[0:N, :] = carry
    state[N : N + 8, :] = jnp.broadcast_to(before, (8, SUB))


def scan_local(x_in, log_decay, b_in, c_in, skip_wide):
    whole = lambda shape: pl.BlockSpec(shape, lambda j: (0, 0))
    return pl.pallas_call(
        local_kernel,
        name="scan_local",
        out_shape=(
            jax.ShapeDtypeStruct((TOK_DEV, SCAN_HEADS * P_SIZE), F32),
            jax.ShapeDtypeStruct((N + 8, SCAN_HEADS * P_SIZE), F32),
            jax.ShapeDtypeStruct((TOK_DEV, SCAN_HEADS), F32),
        ),
        grid=(SCAN_HEADS // 2,),
        in_specs=[
            pl.BlockSpec((TOK_DEV, SUB), lambda j: (0, j)),
            whole((TOK_DEV, SCAN_HEADS)),
            whole((SCAN_HEADS, TOK_DEV)),
            whole((TOK_DEV, N)),
            whole((TOK_DEV, N)),
            pl.BlockSpec((1, SUB), lambda j: (0, j)),
        ],
        out_specs=(
            pl.BlockSpec((TOK_DEV, SUB), lambda j: (0, j)),
            pl.BlockSpec((N + 8, SUB), lambda j: (0, j)),
            whole((TOK_DEV, SCAN_HEADS)),
        ),
        scratch_shapes=[
            pltpu.VMEM((TOK_DEV, 3 * SCAN_HEADS), BF16),
            pltpu.VMEM((SCAN_HEADS, TOK_DEV), F32),
            pltpu.VMEM((TOK_DEV, SUB), F32),
        ],
        compiler_params=pltpu.CompilerParams(vmem_limit_bytes=32 << 20),
    )(x_in, log_decay, jnp.transpose(log_decay), b_in, c_in, skip_wide)


def finish_kernel(part, cum, c, carried, out):
    step = pl.program_id(0)
    width = out.shape[1]
    hi, mid, low = split3(cum[...])
    row = lax.broadcasted_iota(jnp.int32, (3 * SCAN_HEADS, width), 0) % SCAN_HEADS
    lane = lax.broadcasted_iota(jnp.int32, (3 * SCAN_HEADS, width), 1) // P_SIZE
    chosen = (row == lane + step * (width // P_SIZE)).astype(BF16)
    wide = dot_f32(jnp.concatenate([hi, mid, low], axis=1), chosen)
    hi, low = split2(carried[...])
    cs = c[...]
    reach = dot_f32(jnp.concatenate([cs, cs], axis=1), jnp.concatenate([hi, low], axis=0))
    out[...] = (part[...] + jnp.exp(wide) * reach).astype(BF16)


def scan_finish(part, cum, c_in, carried):
    width = 512
    whole = lambda shape: pl.BlockSpec(shape, lambda j: (0, 0))
    column = lambda rows: pl.BlockSpec((rows, width), lambda j: (0, j))
    return pl.pallas_call(
        finish_kernel,
        name="scan_finish",
        out_shape=jax.ShapeDtypeStruct((TOK_DEV, SCAN_HEADS * P_SIZE), BF16),
        grid=(SCAN_HEADS * P_SIZE // width,),
        in_specs=[
            column(TOK_DEV),
            whole((TOK_DEV, SCAN_HEADS)),
            whole((TOK_DEV, N)),
            column(N),
        ],
        out_specs=column(TOK_DEV),
        compiler_params=pltpu.CompilerParams(vmem_limit_bytes=32 << 20),
    )(part, cum, c_in, carried)


def joined(earlier, following):
    total = earlier[N:] + following[N:]
    state = jnp.exp(following[N : N + 1]) * earlier[:N] + following[:N]
    return jnp.concatenate([state, total], axis=0)


def carried_in(own, core, side, plane):
    width = own.shape[1]
    half, quarter = width // 2, width // 4
    mine = jnp.where(core == 0, own[:, :half], own[:, half:])
    other = swapped(jnp.where(core == 0, own[:, half:], own[:, :half]), 1)
    first = jnp.where(core == 0, mine, other)
    second = jnp.where(core == 0, other, mine)
    chip = joined(first, second)
    mine = jnp.where(side == 0, chip[:, :quarter], chip[:, quarter:])
    other = swapped(jnp.where(side == 0, chip[:, quarter:], chip[:, :quarter]), 2)
    lower = jnp.where(side == 0, mine, other)
    upper = jnp.where(side == 0, other, mine)
    total = joined(lower, upper)
    planes = lax.axis_size("ctx") // GROUP
    carry = jnp.zeros_like(total)
    if planes <= 4:
        for back in range(planes - 1, 0, -1):
            came = cyclic(total, GROUP * back)
            carry = jnp.where(plane >= back, joined(carry, came), carry)
    else:
        carry = jnp.where(plane >= 1, cyclic(total, GROUP), carry)
        reach = 1
        while reach < planes:
            came = cyclic(carry, GROUP * reach)
            carry = jnp.where(plane >= reach, joined(came, carry), carry)
            reach *= 2
    after = joined(carry, lower)
    keep = jnp.where(side == 0, carry, after)
    came = swapped(jnp.where(side == 0, after, carry)[:N], 2)
    keep = keep[:N]
    chip_in = jnp.concatenate(
        [jnp.where(side == 0, keep, came), jnp.where(side == 0, came, keep)], axis=1
    )
    next_in = jnp.exp(first[N : N + 1]) * chip_in + first[:N]
    keep = jnp.where(core == 0, chip_in, next_in)
    came = swapped(jnp.where(core == 0, next_in, chip_in), 1)
    return jnp.concatenate(
        [jnp.where(core == 0, keep, came), jnp.where(core == 0, came, keep)], axis=1
    )


def shards(queries, keys, values, x_in, log_decay, b_in, c_in, skip_d):
    device = lax.axis_index("ctx")
    core = device % 2
    side = (device // 2) % 2
    plane = device // GROUP
    flags = jnp.stack(
        [core, side, jnp.where(plane > 0, 1, 0)], axis=0
    ).astype(jnp.int32)
    owns = []
    low = 0
    for heads in CHUNKS:
        cols = slice(low * HD, (low + heads) * HD)
        owns.append(jnp.stack([keys[:, cols], values[:, cols]]))
        low += heads
    befores = [cyclic(own, GROUP) for own in owns]
    near_k, near_v = swapped(keys, 1), swapped(values, 1)
    skip_wide = jnp.repeat(skip_d, P_SIZE)[None, :]
    part, own_state, cum = scan_local(x_in, log_decay, b_in, c_in, skip_wide)
    carried = carried_in(own_state, core, side, plane)
    outs = []
    low = 0
    for heads, own, before in zip(CHUNKS, owns, befores):
        d = swapped(jnp.where(side == 0, own, before), 2)
        e = swapped(before, 1)
        g = swapped(d, 1)
        outs.append(
            attend(flags, low, heads, queries, keys, values, before, d, e, g, near_k, near_v)
        )
        low += heads
    scan_out = scan_finish(part, cum, c_in, carried)
    return (jnp.concatenate(outs, axis=1), scan_out)


def solution(mesh):
    row = P(("seqs", "ctx"), None)
    in_specs = (row,) * 7 + (P(),)
    return jax.shard_map(
        shards, mesh=mesh, in_specs=in_specs, out_specs=(row, row), check_vma=False
    )
```

```python
import functools

import jax
import jax.numpy as jnp
from jax import lax
from jax.experimental import pallas as pl
from jax.experimental.pallas import tpu as pltpu
from jax.sharding import PartitionSpec as P

TOK_DEV = 512
WINDOW = 2048
AH = 16
HD = 128
SCAN_HEADS = 32
P_SIZE = 64
N = 64
GROUP = WINDOW // TOK_DEV
SUB = 128
CHUNKS = (3, 3, 3, 3, 2, 2)
NEG = -1e30
EXP_SCALE = HD ** (-0.5) * 1.4426950408889634
F32 = jnp.float32
BF16 = jnp.bfloat16


def cyclic(array, by):
    count = lax.axis_size("ctx")
    return lax.ppermute(array, "ctx", [(i, (i + by) % count) for i in range(count)])


def swapped(array, bit):
    count = lax.axis_size("ctx")
    return lax.ppermute(array, "ctx", [(i, i ^ bit) for i in range(count)])


def dot_t(a, b):
    return lax.dot_general(a, b, (((1,), (1,)), ((), ())), preferred_element_type=F32)


def dot_v(a, b):
    return lax.dot_general(a, b, (((0,), (0,)), ((), ())), preferred_element_type=F32)


def dot_f32(a, b):
    return jnp.dot(a, b, preferred_element_type=F32)


def attend_kernel(flags, q, k, v, z, d, e, g, xk, xv, *rest):
    out, near = rest[-2:]
    odd, later, full = flags[0], flags[1], flags[2]
    half = TOK_DEV // 2

    @pl.when(odd == 1)
    def _():
        near[0] = xk[...]
        near[1] = xv[...]

    @pl.when(odd == 0)
    def _():
        near[...] = e[...]

    def body(masked):
        q_all = q[...]
        q_lo, q_hi = q[:half, :], q[half:, :]
        key = lax.broadcasted_iota(jnp.int32, (half, half), 0)
        query = lax.broadcasted_iota(jnp.int32, (half, half), 1)
        causal = key <= query
        k_lo, k_hi = k[:half, :], k[half:, :]
        z_lo, z_hi = z[0, :half, :], z[0, half:, :]
        before_lo, before_hi = dot_t(z_lo, q_lo), dot_t(z_hi, q_hi)
        s10 = dot_t(z_hi, q_lo)
        s2, s3, s4 = dot_t(d[0], q_all), dot_t(near[0], q_all), dot_t(g[0], q_all)
        if masked:
            before_lo, before_hi = jnp.full_like(before_lo, NEG), jnp.full_like(before_hi, NEG)
            s10 = jnp.full_like(s10, NEG)
            bias_d = jnp.where(later == 1, 0.0, NEG)
            bias_e = jnp.where(odd == 1, 0.0, NEG)
            s2, s3, s4 = s2 + bias_d, s3 + bias_e, s4 + bias_d
        s00 = jnp.where(causal, dot_t(k_lo, q_lo), before_lo)
        s01 = dot_t(k_lo, q_hi)
        s11 = jnp.where(causal, dot_t(k_hi, q_hi), before_hi)
        most = lambda s: jnp.max(s, axis=0, keepdims=True)
        tri = jnp.concatenate(
            [jnp.maximum(most(s00), most(s10)), jnp.maximum(most(s01), most(s11))], axis=1
        )
        top = jnp.maximum(jnp.maximum(tri, most(s2)), jnp.maximum(most(s3), most(s4)))
        top = top * EXP_SCALE
        t_lo, t_hi = top[:, :half], top[:, half:]
        p00, p10 = jnp.exp2(s00 * EXP_SCALE - t_lo), jnp.exp2(s10 * EXP_SCALE - t_lo)
        p01, p11 = jnp.exp2(s01 * EXP_SCALE - t_hi), jnp.exp2(s11 * EXP_SCALE - t_hi)
        add = lambda p: jnp.sum(p, axis=0, keepdims=True)
        total = jnp.concatenate([add(p00) + add(p10), add(p01) + add(p11)], axis=1)
        mine = lambda p: jnp.where(causal, p, 0.0).astype(BF16)
        theirs = lambda p: jnp.where(causal, 0.0, p).astype(BF16)
        v_lo, v_hi = v[:half, :], v[half:, :]
        w_lo, w_hi = z[1, :half, :], z[1, half:, :]
        acc_lo = dot_v(v_lo, mine(p00)) + dot_v(w_lo, theirs(p00)) + dot_v(w_hi, p10.astype(BF16))
        acc_hi = dot_v(v_hi, mine(p11)) + dot_v(w_hi, theirs(p11)) + dot_v(v_lo, p01.astype(BF16))
        acc = jnp.concatenate([acc_lo, acc_hi], axis=1)
        for s, block in ((s2, d), (s3, near), (s4, g)):
            prob = jnp.exp2(s * EXP_SCALE - top)
            total = total + add(prob)
            acc = acc + dot_v(block[1], prob.astype(BF16))
        out[...] = jnp.transpose(acc / total).astype(BF16)

    @pl.when(full == 1)
    def _():
        body(False)

    @pl.when(full == 0)
    def _():
        body(True)


def attend(flags, low, heads, queries, keys, values, z, d, e, g, xk, xv, sofar):
    wide = pl.BlockSpec((TOK_DEV, HD), lambda j, f: (0, low + j))
    pair = pl.BlockSpec((2, TOK_DEV, HD), lambda j, f: (0, 0, j))
    left = pl.BlockSpec(memory_space=pl.ANY)
    return pl.pallas_call(
        attend_kernel,
        name="attend",
        out_shape=jax.ShapeDtypeStruct((TOK_DEV, AH * HD), BF16),
        grid_spec=pltpu.PrefetchScalarGridSpec(
            num_scalar_prefetch=1,
            grid=(heads,),
            in_specs=[wide, wide, wide, pair, pair, pair, pair, wide, wide] + [left] * len(sofar),
            out_specs=wide,
            scratch_shapes=[pltpu.VMEM((2, TOK_DEV, HD), BF16)],
        ),
        input_output_aliases={10: 0} if sofar else {},
        compiler_params=pltpu.CompilerParams(vmem_limit_bytes=32 << 20),
    )(flags, queries, keys, values, z, d, e, g, xk, xv, *sofar)


def packed(low, heads, keys, values):
    cols = slice(low * HD, (low + heads) * HD)
    return jnp.stack([keys[:, cols], values[:, cols]])


def split3(a):
    hi = a.astype(BF16)
    rest = a - hi.astype(F32)
    mid = rest.astype(BF16)
    low = (rest - mid.astype(F32)).astype(BF16)
    return hi, mid, low


def split2(a):
    hi = a.astype(BF16)
    return hi, (a - hi.astype(F32)).astype(BF16)


def pick(head, width):
    row = lax.broadcasted_iota(jnp.int32, (3 * SCAN_HEADS, width), 0) % SCAN_HEADS
    return (row == head).astype(BF16)


PAIRS = 2


def local_kernel(base, x, decay_t, b_t, c_t, skip, part, state, cum_out, cums, cum_t, cross, b, c):
    step = pl.program_id(0)
    lane = lax.broadcasted_iota(jnp.int32, (SUB, SUB), 1)
    lower = lax.broadcasted_iota(jnp.int32, (SUB, SUB), 0) >= lane
    left = lane < P_SIZE

    @pl.when(step == 0)
    def _():
        t = lax.broadcasted_iota(jnp.int32, (TOK_DEV, TOK_DEV), 0)
        u = lax.broadcasted_iota(jnp.int32, (TOK_DEV, TOK_DEV), 1)
        until = (t <= u).astype(BF16)
        hi, mid, low = split3(decay_t[...])
        total = dot_f32(hi, until) + dot_f32(mid, until) + dot_f32(low, until)
        cum_t[...] = total
        total = jnp.transpose(total)
        cum_out[...] = total
        hi, mid, low = split3(total)
        cums[:, 0:32] = hi
        cums[:, 32:64] = mid
        cums[:, 64:96] = low
        b[...] = jnp.transpose(b_t[...].astype(F32)).astype(BF16)
        c[...] = jnp.transpose(c_t[...].astype(F32)).astype(BF16)
        for s in range(TOK_DEV // SUB):
            at = pl.ds(s * SUB, SUB)
            cross[at, :] = jnp.where(lower, dot_t(c[at, :], b[at, :]), 0.0)

    for pair in range(PAIRS):
        first = 2 * (step * PAIRS + pair) + base
        cols = slice(pair * SUB, (pair + 1) * SUB)
        cum_a = dot_f32(cums[...], pick(first, SUB))
        cum_b = dot_f32(cums[...], pick(first + 1, SUB))
        row_a = cum_t[pl.ds(first, 1), :]
        row_b = cum_t[pl.ds(first + 1, 1), :]
        carry = jnp.zeros((N, SUB), F32)
        before = jnp.zeros((1, SUB), F32)
        for s in range(TOK_DEV // SUB):
            at = slice(s * SUB, (s + 1) * SUB)
            col_a, col_b = cum_a[at, :], cum_b[at, :]
            both = jnp.where(left, col_a, col_b)
            xf = x[at, cols].astype(F32)
            inner = cross[at, :]
            gap_a = jnp.minimum(col_a - row_a[:, at], 0.0)
            gap_b = jnp.minimum(col_b - row_b[:, at], 0.0)
            mix_a = (jnp.exp(gap_a) * inner).astype(BF16)
            mix_b = (jnp.exp(gap_b) * inner).astype(BF16)
            x_a = jnp.where(left, xf, 0.0).astype(BF16)
            x_b = jnp.where(left, 0.0, xf).astype(BF16)
            y = dot_f32(
                jnp.concatenate([mix_a, mix_b], axis=1), jnp.concatenate([x_a, x_b], axis=0)
            )
            if s > 0:
                hi, low = split2(carry)
                cs = c[at, :]
                reach = dot_f32(
                    jnp.concatenate([cs, cs], axis=1), jnp.concatenate([hi, low], axis=0)
                )
                y = y + jnp.exp(both - before) * reach
            part[at, cols] = y + skip[:, cols] * xf
            end = both[SUB - 1 : SUB, :]
            weighted = (xf * jnp.exp(end - both)).astype(BF16)
            added = dot_f32(b_t[:, at], weighted)
            carry = jnp.exp(end - before) * carry + added
            before = end
        state[0:N, cols] = carry
        state[N : N + 8, cols] = jnp.broadcast_to(before, (8, SUB))


def scan_local(half, x_in, decay_t, b_t, c_t, skip_wide):
    width = PAIRS * SUB
    lanes = SCAN_HEADS * P_SIZE // 2
    steps = lanes // width
    whole = lambda shape: pl.BlockSpec(shape, lambda j: (0, 0))
    return pl.pallas_call(
        functools.partial(local_kernel, half * SCAN_HEADS // 2),
        name="scan_local",
        out_shape=(
            jax.ShapeDtypeStruct((TOK_DEV, lanes), F32),
            jax.ShapeDtypeStruct((N + 8, lanes), F32),
            jax.ShapeDtypeStruct((TOK_DEV, SCAN_HEADS), F32),
        ),
        grid=(steps,),
        in_specs=[
            pl.BlockSpec((TOK_DEV, width), lambda j: (0, half * steps + j)),
            whole((SCAN_HEADS, TOK_DEV)),
            whole((N, TOK_DEV)),
            whole((N, TOK_DEV)),
            pl.BlockSpec((1, width), lambda j: (0, half * steps + j)),
        ],
        out_specs=(
            pl.BlockSpec((TOK_DEV, width), lambda j: (0, j)),
            pl.BlockSpec((N + 8, width), lambda j: (0, j)),
            whole((TOK_DEV, SCAN_HEADS)),
        ),
        scratch_shapes=[
            pltpu.VMEM((TOK_DEV, 3 * SCAN_HEADS), BF16),
            pltpu.VMEM((SCAN_HEADS, TOK_DEV), F32),
            pltpu.VMEM((TOK_DEV, SUB), F32),
            pltpu.VMEM((TOK_DEV, N), BF16),
            pltpu.VMEM((TOK_DEV, N), BF16),
        ],
        compiler_params=pltpu.CompilerParams(vmem_limit_bytes=32 << 20),
    )(x_in, decay_t, b_t, c_t, skip_wide)


def finish_kernel(part_a, part_b, cum, c_t, carried, out):
    step = pl.program_id(0)
    part = jnp.where(step < 2, part_a[...], part_b[...])
    width = out.shape[1]
    hi, mid, low = split3(cum[...])
    row = lax.broadcasted_iota(jnp.int32, (3 * SCAN_HEADS, width), 0) % SCAN_HEADS
    lane = lax.broadcasted_iota(jnp.int32, (3 * SCAN_HEADS, width), 1) // P_SIZE
    chosen = (row == lane + step * (width // P_SIZE)).astype(BF16)
    wide = dot_f32(jnp.concatenate([hi, mid, low], axis=1), chosen)
    hi, low = split2(carried[...])
    cs = c_t[...]
    reach = dot_v(jnp.concatenate([cs, cs], axis=0), jnp.concatenate([hi, low], axis=0))
    out[...] = (part + jnp.exp(wide) * reach).astype(BF16)


def scan_finish(part_a, part_b, cum, c_t, carried):
    width = 512
    whole = lambda shape: pl.BlockSpec(shape, lambda j: (0, 0))
    column = lambda rows: pl.BlockSpec((rows, width), lambda j: (0, j))
    return pl.pallas_call(
        finish_kernel,
        name="scan_finish",
        out_shape=jax.ShapeDtypeStruct((TOK_DEV, SCAN_HEADS * P_SIZE), BF16),
        grid=(SCAN_HEADS * P_SIZE // width,),
        in_specs=[
            pl.BlockSpec((TOK_DEV, width), lambda j: (0, jnp.minimum(j, 1))),
            pl.BlockSpec((TOK_DEV, width), lambda j: (0, jnp.maximum(j - 2, 0))),
            whole((TOK_DEV, SCAN_HEADS)),
            whole((N, TOK_DEV)),
            column(N),
        ],
        out_specs=column(TOK_DEV),
        compiler_params=pltpu.CompilerParams(vmem_limit_bytes=32 << 20),
    )(part_a, part_b, cum, c_t, carried)


def joined(earlier, following):
    total = earlier[N:] + following[N:]
    state = jnp.exp(following[N : N + 1]) * earlier[:N] + following[:N]
    return jnp.concatenate([state, total], axis=0)


def after(value, *others):
    return lax.optimization_barrier((value,) + others)[0]


class Carry:
    def __init__(self, state_a, state_b, core, side, plane):
        self.core, self.side, self.plane = core, side, plane
        self.mine = jnp.where(core == 0, state_a, state_b)
        self.other = swapped(jnp.where(core == 0, state_b, state_a), 1)
        self.steps = [self.chip, self.across, self.back, self.spread]

    def advance(self, *others):
        if self.steps:
            self.mine = after(self.mine, *others)
            self.other = after(self.other, *others)
            self.steps.pop(0)()

    def chip(self):
        core, side, quarter = self.core, self.side, self.mine.shape[1] // 2
        self.first = jnp.where(core == 0, self.mine, self.other)
        second = jnp.where(core == 0, self.other, self.mine)
        chip = joined(self.first, second)
        self.mine = jnp.where(side == 0, chip[:, :quarter], chip[:, quarter:])
        self.other = swapped(jnp.where(side == 0, chip[:, quarter:], chip[:, :quarter]), 2)

    def across(self):
        self.lower = jnp.where(self.side == 0, self.mine, self.other)
        upper = jnp.where(self.side == 0, self.other, self.mine)
        total = joined(self.lower, upper)
        planes = lax.axis_size("ctx") // GROUP
        self.mine = total
        if planes <= 4:
            self.other = [cyclic(total, GROUP * back) for back in range(planes - 1, 0, -1)]
        else:
            carry = jnp.where(self.plane >= 1, cyclic(total, GROUP), jnp.zeros_like(total))
            reach = 1
            while reach < planes:
                came = cyclic(carry, GROUP * reach)
                carry = jnp.where(self.plane >= reach, joined(came, carry), carry)
                reach *= 2
            self.other = carry

    def back(self):
        side = self.side
        if isinstance(self.other, list):
            carry = jnp.zeros_like(self.mine)
            for back, came in zip(range(len(self.other), 0, -1), self.other):
                carry = jnp.where(self.plane >= back, joined(carry, came), carry)
        else:
            carry = self.other
        carry = after(carry, self.mine)
        later = joined(carry, self.lower)
        self.mine = jnp.where(side == 0, carry, later)[:N]
        self.other = swapped(jnp.where(side == 0, later, carry)[:N], 2)

    def spread(self):
        core, side, mine, came = self.core, self.side, self.mine, self.other
        chip_in = jnp.concatenate(
            [jnp.where(side == 0, mine, came), jnp.where(side == 0, came, mine)], axis=1
        )
        next_in = jnp.exp(self.first[N : N + 1]) * chip_in + self.first[:N]
        self.mine = jnp.where(core == 0, chip_in, next_in)
        self.other = swapped(jnp.where(core == 0, next_in, chip_in), 1)

    def result(self):
        core, mine, came = self.core, self.mine, self.other
        return jnp.concatenate(
            [jnp.where(core == 0, mine, came), jnp.where(core == 0, came, mine)], axis=1
        )


def shards(queries, keys, values, x_in, log_decay, b_in, c_in, skip_d):
    device = lax.axis_index("ctx")
    core = device % 2
    side = (device // 2) % 2
    plane = device // GROUP
    flags = jnp.stack([core, side, jnp.where(plane > 0, 1, 0)], axis=0).astype(jnp.int32)
    groups = []
    for heads in CHUNKS:
        groups.append((sum(CHUNKS[: len(groups)]), heads))
    count = len(groups)
    own = [packed(*groups[0], keys, values)]
    for group in groups[1:]:
        own.append(packed(*group, after(keys, own[-1]), values))
    before = [cyclic(own[0], GROUP), cyclic(own[1], GROUP), cyclic(own[2], GROUP)]
    near_k, near_v = swapped(after(keys, own[1]), 1), swapped(after(values, own[1]), 1)
    skip_wide = jnp.repeat(skip_d, P_SIZE)[None, :]
    c_t = jnp.transpose(c_in)
    rest = (jnp.transpose(log_decay), jnp.transpose(b_in), c_t, skip_wide)
    part_a, state_a, cum = scan_local(0, after(x_in, own[1]), *rest)

    chosen, across, beside = {}, {}, {}

    def send(k, *others):
        came = after(before[k], *others)
        chosen[k] = jnp.where(side == 0, own[k], came)
        across[k] = swapped(chosen[k], 2)
        beside[k] = swapped(came, 1)
        if k + 3 < count:
            before.append(cyclic(after(own[k + 3], chosen[k]), GROUP))

    send(0, part_a)
    part_b, state_b, _ = scan_local(1, after(x_in, chosen[0]), *rest)
    carry = Carry(state_a, state_b, core, side, plane)
    send(1, part_b)
    out = None
    for k, (low, heads) in enumerate(groups):
        arrived = across[k]
        if k + 1 < count:
            arrived = after(arrived, chosen[k + 1])
        relayed = swapped(arrived, 1)
        if k == count - 1:
            scan_out = scan_finish(part_a, part_b, cum, c_t, after(carry.result(), out))
            relayed = after(relayed, scan_out)
        out = attend(
            flags, low, heads, queries, keys, values, before[k], arrived, beside[k],
            relayed, near_k, near_v, () if k == 0 else (out,),
        )
        if k + 2 < count:
            send(k + 2, out)
        if k in (0, 1, 3, 4):
            carry.advance(out)
    return (out, scan_out)


def solution(mesh):
    row = P(("seqs", "ctx"), None)
    in_specs = (row,) * 7 + (P(),)
    return jax.shard_map(
        shards, mesh=mesh, in_specs=in_specs, out_specs=(row, row), check_vma=False
    )
```

```python
import functools

import jax
import jax.numpy as jnp
from jax import lax
from jax.experimental import pallas as pl
from jax.experimental.pallas import tpu as pltpu
from jax.sharding import PartitionSpec as P

TOK_DEV = 512
WINDOW = 2048
AH = 16
HD = 128
SCAN_HEADS = 32
P_SIZE = 64
N = 64
GROUP = WINDOW // TOK_DEV
SUB = 128
CHUNKS = (4, 4, 3, 3, 2)
STEPS = (0, 1, 2, 3)
NEG = -1e30
EXP_SCALE = HD ** (-0.5) * 1.4426950408889634
F32 = jnp.float32
BF16 = jnp.bfloat16


def cyclic(array, by):
    count = lax.axis_size("ctx")
    return lax.ppermute(array, "ctx", [(i, (i + by) % count) for i in range(count)])


def swapped(array, bit):
    count = lax.axis_size("ctx")
    return lax.ppermute(array, "ctx", [(i, i ^ bit) for i in range(count)])


def dot_t(a, b):
    return lax.dot_general(a, b, (((1,), (1,)), ((), ())), preferred_element_type=F32)


def dot_v(a, b):
    return lax.dot_general(a, b, (((0,), (0,)), ((), ())), preferred_element_type=F32)


def dot_f32(a, b):
    return jnp.dot(a, b, preferred_element_type=F32)


def attend_kernel(flags, q, k, v, z, d, e, g, xk, xv, *rest):
    out, near = rest[-2:]
    odd, later, full = flags[0], flags[1], flags[2]
    half = TOK_DEV // 2

    @pl.when(odd == 1)
    def _():
        near[0] = xk[...]
        near[1] = xv[...]

    @pl.when(odd == 0)
    def _():
        near[...] = e[...]

    def body(masked):
        q_all = q[...]
        q_lo, q_hi = q[:half, :], q[half:, :]
        key = lax.broadcasted_iota(jnp.int32, (half, half), 0)
        query = lax.broadcasted_iota(jnp.int32, (half, half), 1)
        causal = key <= query
        k_lo, k_hi = k[:half, :], k[half:, :]
        z_lo, z_hi = z[0, :half, :], z[0, half:, :]
        before_lo, before_hi = dot_t(z_lo, q_lo), dot_t(z_hi, q_hi)
        s10 = dot_t(z_hi, q_lo)
        s2, s3, s4 = dot_t(d[0], q_all), dot_t(near[0], q_all), dot_t(g[0], q_all)
        if masked:
            before_lo, before_hi = jnp.full_like(before_lo, NEG), jnp.full_like(before_hi, NEG)
            s10 = jnp.full_like(s10, NEG)
            bias_d = jnp.where(later == 1, 0.0, NEG)
            bias_e = jnp.where(odd == 1, 0.0, NEG)
            s2, s3, s4 = s2 + bias_d, s3 + bias_e, s4 + bias_d
        s00 = jnp.where(causal, dot_t(k_lo, q_lo), before_lo)
        s01 = dot_t(k_lo, q_hi)
        s11 = jnp.where(causal, dot_t(k_hi, q_hi), before_hi)
        most = lambda s: jnp.max(s, axis=0, keepdims=True)
        tri = jnp.concatenate(
            [jnp.maximum(most(s00), most(s10)), jnp.maximum(most(s01), most(s11))], axis=1
        )
        top = jnp.maximum(jnp.maximum(tri, most(s2)), jnp.maximum(most(s3), most(s4)))
        top = top * EXP_SCALE
        t_lo, t_hi = top[:, :half], top[:, half:]
        p00, p10 = jnp.exp2(s00 * EXP_SCALE - t_lo), jnp.exp2(s10 * EXP_SCALE - t_lo)
        p01, p11 = jnp.exp2(s01 * EXP_SCALE - t_hi), jnp.exp2(s11 * EXP_SCALE - t_hi)
        add = lambda p: jnp.sum(p, axis=0, keepdims=True)
        total = jnp.concatenate([add(p00) + add(p10), add(p01) + add(p11)], axis=1)
        mine = lambda p: jnp.where(causal, p, 0.0).astype(BF16)
        theirs = lambda p: jnp.where(causal, 0.0, p).astype(BF16)
        v_lo, v_hi = v[:half, :], v[half:, :]
        w_lo, w_hi = z[1, :half, :], z[1, half:, :]
        acc_lo = dot_v(v_lo, mine(p00)) + dot_v(w_lo, theirs(p00)) + dot_v(w_hi, p10.astype(BF16))
        acc_hi = dot_v(v_hi, mine(p11)) + dot_v(w_hi, theirs(p11)) + dot_v(v_lo, p01.astype(BF16))
        acc = jnp.concatenate([acc_lo, acc_hi], axis=1)
        for s, block in ((s2, d), (s3, near), (s4, g)):
            prob = jnp.exp2(s * EXP_SCALE - top)
            total = total + add(prob)
            acc = acc + dot_v(block[1], prob.astype(BF16))
        out[...] = jnp.transpose(acc / total).astype(BF16)

    @pl.when(full == 1)
    def _():
        body(False)

    @pl.when(full == 0)
    def _():
        body(True)


def attend(flags, low, heads, queries, keys, values, z, d, e, g, xk, xv, sofar):
    wide = pl.BlockSpec((TOK_DEV, HD), lambda j, f: (0, low + j))
    pair = pl.BlockSpec((2, TOK_DEV, HD), lambda j, f: (0, 0, j))
    left = pl.BlockSpec(memory_space=pl.ANY)
    return pl.pallas_call(
        attend_kernel,
        name="attend",
        out_shape=jax.ShapeDtypeStruct((TOK_DEV, AH * HD), BF16),
        grid_spec=pltpu.PrefetchScalarGridSpec(
            num_scalar_prefetch=1,
            grid=(heads,),
            in_specs=[wide, wide, wide, pair, pair, pair, pair, wide, wide] + [left] * len(sofar),
            out_specs=wide,
            scratch_shapes=[pltpu.VMEM((2, TOK_DEV, HD), BF16)],
        ),
        input_output_aliases={10: 0} if sofar else {},
        compiler_params=pltpu.CompilerParams(vmem_limit_bytes=32 << 20),
    )(flags, queries, keys, values, z, d, e, g, xk, xv, *sofar)


def packed(low, heads, keys, values):
    cols = slice(low * HD, (low + heads) * HD)
    return jnp.stack([keys[:, cols], values[:, cols]])


def split3(a):
    hi = a.astype(BF16)
    rest = a - hi.astype(F32)
    mid = rest.astype(BF16)
    low = (rest - mid.astype(F32)).astype(BF16)
    return hi, mid, low


def split2(a):
    hi = a.astype(BF16)
    return hi, (a - hi.astype(F32)).astype(BF16)


def pick(head, width):
    row = lax.broadcasted_iota(jnp.int32, (3 * SCAN_HEADS, width), 0) % SCAN_HEADS
    return (row == head).astype(BF16)


PAIRS = 2


def local_kernel(base, x, decay_t, b_t, c_t, skip, part, state, cum_out, cums, cum_t, cross, b, c):
    step = pl.program_id(0)
    lane = lax.broadcasted_iota(jnp.int32, (SUB, SUB), 1)
    lower = lax.broadcasted_iota(jnp.int32, (SUB, SUB), 0) >= lane
    left = lane < P_SIZE

    @pl.when(step == 0)
    def _():
        t = lax.broadcasted_iota(jnp.int32, (TOK_DEV, TOK_DEV), 0)
        u = lax.broadcasted_iota(jnp.int32, (TOK_DEV, TOK_DEV), 1)
        until = (t <= u).astype(BF16)
        hi, mid, low = split3(decay_t[...])
        total = dot_f32(hi, until) + dot_f32(mid, until) + dot_f32(low, until)
        cum_t[...] = total
        total = jnp.transpose(total)
        cum_out[...] = total
        hi, mid, low = split3(total)
        cums[:, 0:32] = hi
        cums[:, 32:64] = mid
        cums[:, 64:96] = low
        b[...] = jnp.transpose(b_t[...].astype(F32)).astype(BF16)
        c[...] = jnp.transpose(c_t[...].astype(F32)).astype(BF16)
        for s in range(TOK_DEV // SUB):
            at = pl.ds(s * SUB, SUB)
            cross[at, :] = jnp.where(lower, dot_t(c[at, :], b[at, :]), 0.0)

    for pair in range(PAIRS):
        first = 2 * (step * PAIRS + pair) + base
        cols = slice(pair * SUB, (pair + 1) * SUB)
        cum_a = dot_f32(cums[...], pick(first, SUB))
        cum_b = dot_f32(cums[...], pick(first + 1, SUB))
        row_a = cum_t[pl.ds(first, 1), :]
        row_b = cum_t[pl.ds(first + 1, 1), :]
        carry = jnp.zeros((N, SUB), F32)
        before = jnp.zeros((1, SUB), F32)
        for s in range(TOK_DEV // SUB):
            at = slice(s * SUB, (s + 1) * SUB)
            col_a, col_b = cum_a[at, :], cum_b[at, :]
            both = jnp.where(left, col_a, col_b)
            xf = x[at, cols].astype(F32)
            inner = cross[at, :]
            gap_a = jnp.minimum(col_a - row_a[:, at], 0.0)
            gap_b = jnp.minimum(col_b - row_b[:, at], 0.0)
            mix_a = (jnp.exp(gap_a) * inner).astype(BF16)
            mix_b = (jnp.exp(gap_b) * inner).astype(BF16)
            x_a = jnp.where(left, xf, 0.0).astype(BF16)
            x_b = jnp.where(left, 0.0, xf).astype(BF16)
            y = dot_f32(
                jnp.concatenate([mix_a, mix_b], axis=1), jnp.concatenate([x_a, x_b], axis=0)
            )
            if s > 0:
                hi, low = split2(carry)
                cs = c[at, :]
                reach = dot_f32(
                    jnp.concatenate([cs, cs], axis=1), jnp.concatenate([hi, low], axis=0)
                )
                y = y + jnp.exp(both - before) * reach
            part[at, cols] = y + skip[:, cols] * xf
            end = both[SUB - 1 : SUB, :]
            weighted = (xf * jnp.exp(end - both)).astype(BF16)
            added = dot_f32(b_t[:, at], weighted)
            carry = jnp.exp(end - before) * carry + added
            before = end
        state[0:N, cols] = carry
        state[N : N + 8, cols] = jnp.broadcast_to(before, (8, SUB))


def scan_local(half, x_in, decay_t, b_t, c_t, skip_wide):
    width = PAIRS * SUB
    lanes = SCAN_HEADS * P_SIZE // 2
    steps = lanes // width
    whole = lambda shape: pl.BlockSpec(shape, lambda j: (0, 0))
    return pl.pallas_call(
        functools.partial(local_kernel, half * SCAN_HEADS // 2),
        name="scan_local",
        out_shape=(
            jax.ShapeDtypeStruct((TOK_DEV, lanes), F32),
            jax.ShapeDtypeStruct((N + 8, lanes), F32),
            jax.ShapeDtypeStruct((TOK_DEV, SCAN_HEADS), F32),
        ),
        grid=(steps,),
        in_specs=[
            pl.BlockSpec((TOK_DEV, width), lambda j: (0, half * steps + j)),
            whole((SCAN_HEADS, TOK_DEV)),
            whole((N, TOK_DEV)),
            whole((N, TOK_DEV)),
            pl.BlockSpec((1, width), lambda j: (0, half * steps + j)),
        ],
        out_specs=(
            pl.BlockSpec((TOK_DEV, width), lambda j: (0, j)),
            pl.BlockSpec((N + 8, width), lambda j: (0, j)),
            whole((TOK_DEV, SCAN_HEADS)),
        ),
        scratch_shapes=[
            pltpu.VMEM((TOK_DEV, 3 * SCAN_HEADS), BF16),
            pltpu.VMEM((SCAN_HEADS, TOK_DEV), F32),
            pltpu.VMEM((TOK_DEV, SUB), F32),
            pltpu.VMEM((TOK_DEV, N), BF16),
            pltpu.VMEM((TOK_DEV, N), BF16),
        ],
        compiler_params=pltpu.CompilerParams(vmem_limit_bytes=32 << 20),
    )(x_in, decay_t, b_t, c_t, skip_wide)


def finish_kernel(part_a, part_b, cum, c_t, carried, out):
    step = pl.program_id(0)
    part = jnp.where(step < 2, part_a[...], part_b[...])
    width = out.shape[1]
    hi, mid, low = split3(cum[...])
    row = lax.broadcasted_iota(jnp.int32, (3 * SCAN_HEADS, width), 0) % SCAN_HEADS
    lane = lax.broadcasted_iota(jnp.int32, (3 * SCAN_HEADS, width), 1) // P_SIZE
    chosen = (row == lane + step * (width // P_SIZE)).astype(BF16)
    wide = dot_f32(jnp.concatenate([hi, mid, low], axis=1), chosen)
    hi, low = split2(carried[...])
    cs = c_t[...]
    reach = dot_v(jnp.concatenate([cs, cs], axis=0), jnp.concatenate([hi, low], axis=0))
    out[...] = (part + jnp.exp(wide) * reach).astype(BF16)


def scan_finish(part_a, part_b, cum, c_t, carried):
    width = 512
    whole = lambda shape: pl.BlockSpec(shape, lambda j: (0, 0))
    column = lambda rows: pl.BlockSpec((rows, width), lambda j: (0, j))
    return pl.pallas_call(
        finish_kernel,
        name="scan_finish",
        out_shape=jax.ShapeDtypeStruct((TOK_DEV, SCAN_HEADS * P_SIZE), BF16),
        grid=(SCAN_HEADS * P_SIZE // width,),
        in_specs=[
            pl.BlockSpec((TOK_DEV, width), lambda j: (0, jnp.minimum(j, 1))),
            pl.BlockSpec((TOK_DEV, width), lambda j: (0, jnp.maximum(j - 2, 0))),
            whole((TOK_DEV, SCAN_HEADS)),
            whole((N, TOK_DEV)),
            column(N),
        ],
        out_specs=column(TOK_DEV),
        compiler_params=pltpu.CompilerParams(vmem_limit_bytes=32 << 20),
    )(part_a, part_b, cum, c_t, carried)


def joined(earlier, following):
    total = earlier[N:] + following[N:]
    state = jnp.exp(following[N : N + 1]) * earlier[:N] + following[:N]
    return jnp.concatenate([state, total], axis=0)


def after(value, *others):
    return lax.optimization_barrier((value,) + others)[0]


class Carry:
    def __init__(self, state_a, state_b, core, side, plane):
        self.core, self.side, self.plane = core, side, plane
        self.mine = jnp.where(core == 0, state_a, state_b)
        self.other = swapped(jnp.where(core == 0, state_b, state_a), 1)
        self.steps = [self.chip, self.across, self.back, self.spread]

    def advance(self, *others):
        if self.steps:
            self.mine = after(self.mine, *others)
            self.other = after(self.other, *others)
            self.steps.pop(0)()

    def chip(self):
        core, side, quarter = self.core, self.side, self.mine.shape[1] // 2
        self.first = jnp.where(core == 0, self.mine, self.other)
        second = jnp.where(core == 0, self.other, self.mine)
        chip = joined(self.first, second)
        self.mine = jnp.where(side == 0, chip[:, :quarter], chip[:, quarter:])
        self.other = swapped(jnp.where(side == 0, chip[:, quarter:], chip[:, :quarter]), 2)

    def across(self):
        self.lower = jnp.where(self.side == 0, self.mine, self.other)
        upper = jnp.where(self.side == 0, self.other, self.mine)
        total = joined(self.lower, upper)
        planes = lax.axis_size("ctx") // GROUP
        self.mine = total
        if planes <= 4:
            self.other = [cyclic(total, GROUP * back) for back in range(planes - 1, 0, -1)]
        else:
            carry = jnp.where(self.plane >= 1, cyclic(total, GROUP), jnp.zeros_like(total))
            reach = 1
            while reach < planes:
                came = cyclic(carry, GROUP * reach)
                carry = jnp.where(self.plane >= reach, joined(came, carry), carry)
                reach *= 2
            self.other = carry

    def back(self):
        side = self.side
        if isinstance(self.other, list):
            carry = jnp.zeros_like(self.mine)
            for back, came in zip(range(len(self.other), 0, -1), self.other):
                carry = jnp.where(self.plane >= back, joined(carry, came), carry)
        else:
            carry = self.other
        carry = after(carry, self.mine)
        later = joined(carry, self.lower)
        self.mine = jnp.where(side == 0, carry, later)[:N]
        self.other = swapped(jnp.where(side == 0, later, carry)[:N], 2)

    def spread(self):
        core, side, mine, came = self.core, self.side, self.mine, self.other
        chip_in = jnp.concatenate(
            [jnp.where(side == 0, mine, came), jnp.where(side == 0, came, mine)], axis=1
        )
        next_in = jnp.exp(self.first[N : N + 1]) * chip_in + self.first[:N]
        self.mine = jnp.where(core == 0, chip_in, next_in)
        self.other = swapped(jnp.where(core == 0, next_in, chip_in), 1)

    def result(self):
        core, mine, came = self.core, self.mine, self.other
        return jnp.concatenate(
            [jnp.where(core == 0, mine, came), jnp.where(core == 0, came, mine)], axis=1
        )


def shards(queries, keys, values, x_in, log_decay, b_in, c_in, skip_d):
    device = lax.axis_index("ctx")
    core = device % 2
    side = (device // 2) % 2
    plane = device // GROUP
    flags = jnp.stack([core, side, jnp.where(plane > 0, 1, 0)], axis=0).astype(jnp.int32)
    groups = []
    for heads in CHUNKS:
        groups.append((sum(CHUNKS[: len(groups)]), heads))
    count = len(groups)
    own = [packed(*groups[0], keys, values)]
    for group in groups[1:]:
        own.append(packed(*group, after(keys, own[-1]), values))
    before = [cyclic(own[0], GROUP), cyclic(own[1], GROUP), cyclic(own[2], GROUP)]
    near_k, near_v = swapped(after(keys, own[1]), 1), swapped(after(values, own[1]), 1)
    skip_wide = jnp.repeat(skip_d, P_SIZE)[None, :]
    c_t = jnp.transpose(c_in)
    rest = (jnp.transpose(log_decay), jnp.transpose(b_in), c_t, skip_wide)
    part_a, state_a, cum = scan_local(0, after(x_in, own[1]), *rest)

    chosen, across, beside = {}, {}, {}

    def send(k, *others):
        came = after(before[k], *others)
        chosen[k] = jnp.where(side == 0, own[k], came)
        across[k] = swapped(chosen[k], 2)
        beside[k] = swapped(came, 1)
        if k + 3 < count:
            before.append(cyclic(after(own[k + 3], chosen[k]), GROUP))

    send(0, part_a)
    part_b, state_b, _ = scan_local(1, after(x_in, chosen[0]), *rest)
    carry = Carry(state_a, state_b, core, side, plane)
    send(1, part_b)
    out = None
    for k, (low, heads) in enumerate(groups):
        arrived = across[k]
        if k + 1 < count:
            arrived = after(arrived, chosen[k + 1])
        relayed = swapped(arrived, 1)
        if k == count - 1:
            scan_out = scan_finish(part_a, part_b, cum, c_t, after(carry.result(), out))
            relayed = after(relayed, scan_out)
        out = attend(
            flags, low, heads, queries, keys, values, before[k], arrived, beside[k],
            relayed, near_k, near_v, () if k == 0 else (out,),
        )
        if k + 2 < count:
            send(k + 2, out)
        if k in STEPS:
            carry.advance(out)
    return (out, scan_out)


def solution(mesh):
    row = P(("seqs", "ctx"), None)
    in_specs = (row,) * 7 + (P(),)
    return jax.shard_map(
        shards, mesh=mesh, in_specs=in_specs, out_specs=(row, row), check_vma=False
    )
```

```python
import functools

import jax
import jax.numpy as jnp
from jax import lax
from jax.experimental import pallas as pl
from jax.experimental.pallas import tpu as pltpu
from jax.sharding import PartitionSpec as P

TOK_DEV = 512
WINDOW = 2048
AH = 16
HD = 128
SCAN_HEADS = 32
P_SIZE = 64
N = 64
GROUP = WINDOW // TOK_DEV
SUB = 128
CHUNKS = (4, 4, 3, 3, 2)
STEPS = (0, 1, 2, 3)
NEG = -1e30
EXP_SCALE = HD ** (-0.5) * 1.4426950408889634
F32 = jnp.float32
BF16 = jnp.bfloat16


def in_hbm(*arrays):
    return [pltpu.with_memory_space_constraint(array, pltpu.HBM) for array in arrays]


def cyclic(array, by):
    count = lax.axis_size("ctx")
    return lax.ppermute(array, "ctx", [(i, (i + by) % count) for i in range(count)])


def swapped(array, bit):
    count = lax.axis_size("ctx")
    return lax.ppermute(array, "ctx", [(i, i ^ bit) for i in range(count)])


def dot_t(a, b):
    return lax.dot_general(a, b, (((1,), (1,)), ((), ())), preferred_element_type=F32)


def dot_v(a, b):
    return lax.dot_general(a, b, (((0,), (0,)), ((), ())), preferred_element_type=F32)


def dot_f32(a, b):
    return jnp.dot(a, b, preferred_element_type=F32)


def attend_kernel(flags, q, k, v, z, d, e, g, xk, xv, *rest):
    out, near = rest[-2:]
    odd, later, full = flags[0], flags[1], flags[2]
    half = TOK_DEV // 2

    @pl.when(odd == 1)
    def _():
        near[0] = xk[...]
        near[1] = xv[...]

    @pl.when(odd == 0)
    def _():
        near[...] = e[...]

    def body(masked):
        q_all = q[...]
        q_lo, q_hi = q[:half, :], q[half:, :]
        key = lax.broadcasted_iota(jnp.int32, (half, half), 0)
        query = lax.broadcasted_iota(jnp.int32, (half, half), 1)
        causal = key <= query
        k_lo, k_hi = k[:half, :], k[half:, :]
        z_lo, z_hi = z[0, :half, :], z[0, half:, :]
        before_lo, before_hi = dot_t(z_lo, q_lo), dot_t(z_hi, q_hi)
        s10 = dot_t(z_hi, q_lo)
        s2, s3, s4 = dot_t(d[0], q_all), dot_t(near[0], q_all), dot_t(g[0], q_all)
        if masked:
            before_lo, before_hi = jnp.full_like(before_lo, NEG), jnp.full_like(before_hi, NEG)
            s10 = jnp.full_like(s10, NEG)
            bias_d = jnp.where(later == 1, 0.0, NEG)
            bias_e = jnp.where(odd == 1, 0.0, NEG)
            s2, s3, s4 = s2 + bias_d, s3 + bias_e, s4 + bias_d
        s00 = jnp.where(causal, dot_t(k_lo, q_lo), before_lo)
        s01 = dot_t(k_lo, q_hi)
        s11 = jnp.where(causal, dot_t(k_hi, q_hi), before_hi)
        most = lambda s: jnp.max(s, axis=0, keepdims=True)
        tri = jnp.concatenate(
            [jnp.maximum(most(s00), most(s10)), jnp.maximum(most(s01), most(s11))], axis=1
        )
        top = jnp.maximum(jnp.maximum(tri, most(s2)), jnp.maximum(most(s3), most(s4)))
        top = top * EXP_SCALE
        t_lo, t_hi = top[:, :half], top[:, half:]
        p00, p10 = jnp.exp2(s00 * EXP_SCALE - t_lo), jnp.exp2(s10 * EXP_SCALE - t_lo)
        p01, p11 = jnp.exp2(s01 * EXP_SCALE - t_hi), jnp.exp2(s11 * EXP_SCALE - t_hi)
        add = lambda p: jnp.sum(p, axis=0, keepdims=True)
        total = jnp.concatenate([add(p00) + add(p10), add(p01) + add(p11)], axis=1)
        mine = lambda p: jnp.where(causal, p, 0.0).astype(BF16)
        theirs = lambda p: jnp.where(causal, 0.0, p).astype(BF16)
        v_lo, v_hi = v[:half, :], v[half:, :]
        w_lo, w_hi = z[1, :half, :], z[1, half:, :]
        acc_lo = dot_v(v_lo, mine(p00)) + dot_v(w_lo, theirs(p00)) + dot_v(w_hi, p10.astype(BF16))
        acc_hi = dot_v(v_hi, mine(p11)) + dot_v(w_hi, theirs(p11)) + dot_v(v_lo, p01.astype(BF16))
        acc = jnp.concatenate([acc_lo, acc_hi], axis=1)
        for s, block in ((s2, d), (s3, near), (s4, g)):
            prob = jnp.exp2(s * EXP_SCALE - top)
            total = total + add(prob)
            acc = acc + dot_v(block[1], prob.astype(BF16))
        out[...] = jnp.transpose(acc / total).astype(BF16)

    @pl.when(full == 1)
    def _():
        body(False)

    @pl.when(full == 0)
    def _():
        body(True)


def attend(flags, low, heads, queries, keys, values, z, d, e, g, xk, xv, sofar):
    wide = pl.BlockSpec((TOK_DEV, HD), lambda j, f: (0, low + j))
    pair = pl.BlockSpec((2, TOK_DEV, HD), lambda j, f: (0, 0, j))
    left = pl.BlockSpec(memory_space=pl.ANY)
    return pl.pallas_call(
        attend_kernel,
        name="attend",
        out_shape=jax.ShapeDtypeStruct((TOK_DEV, AH * HD), BF16),
        grid_spec=pltpu.PrefetchScalarGridSpec(
            num_scalar_prefetch=1,
            grid=(heads,),
            in_specs=[wide, wide, wide, pair, pair, pair, pair, wide, wide] + [left] * len(sofar),
            out_specs=wide,
            scratch_shapes=[pltpu.VMEM((2, TOK_DEV, HD), BF16)],
        ),
        input_output_aliases={10: 0} if sofar else {},
        compiler_params=pltpu.CompilerParams(vmem_limit_bytes=32 << 20),
    )(flags, *in_hbm(queries, keys, values), z, d, e, g, *in_hbm(xk, xv), *sofar)


def packed(low, heads, keys, values):
    cols = slice(low * HD, (low + heads) * HD)
    return jnp.stack([keys[:, cols], values[:, cols]])


def split3(a):
    hi = a.astype(BF16)
    rest = a - hi.astype(F32)
    mid = rest.astype(BF16)
    low = (rest - mid.astype(F32)).astype(BF16)
    return hi, mid, low


def split2(a):
    hi = a.astype(BF16)
    return hi, (a - hi.astype(F32)).astype(BF16)


def pick(head, width):
    row = lax.broadcasted_iota(jnp.int32, (3 * SCAN_HEADS, width), 0) % SCAN_HEADS
    return (row == head).astype(BF16)


PAIRS = 2


def local_kernel(base, x, decay_t, b_t, c_t, skip, part, state, cum_out, cums, cum_t, cross, b, c):
    step = pl.program_id(0)
    lane = lax.broadcasted_iota(jnp.int32, (SUB, SUB), 1)
    lower = lax.broadcasted_iota(jnp.int32, (SUB, SUB), 0) >= lane
    left = lane < P_SIZE

    @pl.when(step == 0)
    def _():
        t = lax.broadcasted_iota(jnp.int32, (TOK_DEV, TOK_DEV), 0)
        u = lax.broadcasted_iota(jnp.int32, (TOK_DEV, TOK_DEV), 1)
        until = (t <= u).astype(BF16)
        hi, mid, low = split3(decay_t[...])
        total = dot_f32(hi, until) + dot_f32(mid, until) + dot_f32(low, until)
        cum_t[...] = total
        total = jnp.transpose(total)
        cum_out[...] = total
        hi, mid, low = split3(total)
        cums[:, 0:32] = hi
        cums[:, 32:64] = mid
        cums[:, 64:96] = low
        b[...] = jnp.transpose(b_t[...].astype(F32)).astype(BF16)
        c[...] = jnp.transpose(c_t[...].astype(F32)).astype(BF16)
        for s in range(TOK_DEV // SUB):
            at = pl.ds(s * SUB, SUB)
            cross[at, :] = jnp.where(lower, dot_t(c[at, :], b[at, :]), 0.0)

    for pair in range(PAIRS):
        first = 2 * (step * PAIRS + pair) + base
        cols = slice(pair * SUB, (pair + 1) * SUB)
        cum_a = dot_f32(cums[...], pick(first, SUB))
        cum_b = dot_f32(cums[...], pick(first + 1, SUB))
        row_a = cum_t[pl.ds(first, 1), :]
        row_b = cum_t[pl.ds(first + 1, 1), :]
        carry = jnp.zeros((N, SUB), F32)
        before = jnp.zeros((1, SUB), F32)
        for s in range(TOK_DEV // SUB):
            at = slice(s * SUB, (s + 1) * SUB)
            col_a, col_b = cum_a[at, :], cum_b[at, :]
            both = jnp.where(left, col_a, col_b)
            xf = x[at, cols].astype(F32)
            inner = cross[at, :]
            gap_a = jnp.minimum(col_a - row_a[:, at], 0.0)
            gap_b = jnp.minimum(col_b - row_b[:, at], 0.0)
            mix_a = (jnp.exp(gap_a) * inner).astype(BF16)
            mix_b = (jnp.exp(gap_b) * inner).astype(BF16)
            x_a = jnp.where(left, xf, 0.0).astype(BF16)
            x_b = jnp.where(left, 0.0, xf).astype(BF16)
            y = dot_f32(
                jnp.concatenate([mix_a, mix_b], axis=1), jnp.concatenate([x_a, x_b], axis=0)
            )
            if s > 0:
                hi, low = split2(carry)
                cs = c[at, :]
                reach = dot_f32(
                    jnp.concatenate([cs, cs], axis=1), jnp.concatenate([hi, low], axis=0)
                )
                y = y + jnp.exp(both - before) * reach
            part[at, cols] = y + skip[:, cols] * xf
            end = both[SUB - 1 : SUB, :]
            weighted = (xf * jnp.exp(end - both)).astype(BF16)
            added = dot_f32(b_t[:, at], weighted)
            carry = jnp.exp(end - before) * carry + added
            before = end
        state[0:N, cols] = carry
        state[N : N + 8, cols] = jnp.broadcast_to(before, (8, SUB))


def scan_local(half, x_in, decay_t, b_t, c_t, skip_wide):
    width = PAIRS * SUB
    lanes = SCAN_HEADS * P_SIZE // 2
    steps = lanes // width
    whole = lambda shape: pl.BlockSpec(shape, lambda j: (0, 0))
    return pl.pallas_call(
        functools.partial(local_kernel, half * SCAN_HEADS // 2),
        name="scan_local",
        out_shape=(
            pltpu.HBM((TOK_DEV, lanes), F32),
            jax.ShapeDtypeStruct((N + 8, lanes), F32),
            jax.ShapeDtypeStruct((TOK_DEV, SCAN_HEADS), F32),
        ),
        grid=(steps,),
        in_specs=[
            pl.BlockSpec((TOK_DEV, width), lambda j: (0, half * steps + j)),
            whole((SCAN_HEADS, TOK_DEV)),
            whole((N, TOK_DEV)),
            whole((N, TOK_DEV)),
            pl.BlockSpec((1, width), lambda j: (0, half * steps + j)),
        ],
        out_specs=(
            pl.BlockSpec((TOK_DEV, width), lambda j: (0, j)),
            pl.BlockSpec((N + 8, width), lambda j: (0, j)),
            whole((TOK_DEV, SCAN_HEADS)),
        ),
        scratch_shapes=[
            pltpu.VMEM((TOK_DEV, 3 * SCAN_HEADS), BF16),
            pltpu.VMEM((SCAN_HEADS, TOK_DEV), F32),
            pltpu.VMEM((TOK_DEV, SUB), F32),
            pltpu.VMEM((TOK_DEV, N), BF16),
            pltpu.VMEM((TOK_DEV, N), BF16),
        ],
        compiler_params=pltpu.CompilerParams(vmem_limit_bytes=32 << 20),
    )(*in_hbm(x_in), decay_t, b_t, c_t, skip_wide)


def finish_kernel(part_a, part_b, cum, c_t, carried, out):
    step = pl.program_id(0)
    part = jnp.where(step < 2, part_a[...], part_b[...])
    width = out.shape[1]
    hi, mid, low = split3(cum[...])
    row = lax.broadcasted_iota(jnp.int32, (3 * SCAN_HEADS, width), 0) % SCAN_HEADS
    lane = lax.broadcasted_iota(jnp.int32, (3 * SCAN_HEADS, width), 1) // P_SIZE
    chosen = (row == lane + step * (width // P_SIZE)).astype(BF16)
    wide = dot_f32(jnp.concatenate([hi, mid, low], axis=1), chosen)
    hi, low = split2(carried[...])
    cs = c_t[...]
    reach = dot_v(jnp.concatenate([cs, cs], axis=0), jnp.concatenate([hi, low], axis=0))
    out[...] = (part + jnp.exp(wide) * reach).astype(BF16)


def scan_finish(part_a, part_b, cum, c_t, carried):
    width = 512
    whole = lambda shape: pl.BlockSpec(shape, lambda j: (0, 0))
    column = lambda rows: pl.BlockSpec((rows, width), lambda j: (0, j))
    return pl.pallas_call(
        finish_kernel,
        name="scan_finish",
        out_shape=jax.ShapeDtypeStruct((TOK_DEV, SCAN_HEADS * P_SIZE), BF16),
        grid=(SCAN_HEADS * P_SIZE // width,),
        in_specs=[
            pl.BlockSpec((TOK_DEV, width), lambda j: (0, jnp.minimum(j, 1))),
            pl.BlockSpec((TOK_DEV, width), lambda j: (0, jnp.maximum(j - 2, 0))),
            whole((TOK_DEV, SCAN_HEADS)),
            whole((N, TOK_DEV)),
            column(N),
        ],
        out_specs=column(TOK_DEV),
        compiler_params=pltpu.CompilerParams(vmem_limit_bytes=32 << 20),
    )(*in_hbm(part_a, part_b), cum, c_t, carried)


def joined(earlier, following):
    total = earlier[N:] + following[N:]
    state = jnp.exp(following[N : N + 1]) * earlier[:N] + following[:N]
    return jnp.concatenate([state, total], axis=0)


def after(value, *others):
    return lax.optimization_barrier((value,) + others)[0]


class Carry:
    def __init__(self, state_a, state_b, core, side, plane):
        self.core, self.side, self.plane = core, side, plane
        self.mine = jnp.where(core == 0, state_a, state_b)
        self.other = swapped(jnp.where(core == 0, state_b, state_a), 1)
        self.steps = [self.chip, self.across, self.back, self.spread]

    def advance(self, *others):
        if self.steps:
            self.mine = after(self.mine, *others)
            self.other = after(self.other, *others)
            self.steps.pop(0)()

    def chip(self):
        core, side, quarter = self.core, self.side, self.mine.shape[1] // 2
        self.first = jnp.where(core == 0, self.mine, self.other)
        second = jnp.where(core == 0, self.other, self.mine)
        chip = joined(self.first, second)
        self.mine = jnp.where(side == 0, chip[:, :quarter], chip[:, quarter:])
        self.other = swapped(jnp.where(side == 0, chip[:, quarter:], chip[:, :quarter]), 2)

    def across(self):
        self.lower = jnp.where(self.side == 0, self.mine, self.other)
        upper = jnp.where(self.side == 0, self.other, self.mine)
        total = joined(self.lower, upper)
        planes = lax.axis_size("ctx") // GROUP
        self.mine = total
        if planes <= 4:
            self.other = [cyclic(total, GROUP * back) for back in range(planes - 1, 0, -1)]
        else:
            carry = jnp.where(self.plane >= 1, cyclic(total, GROUP), jnp.zeros_like(total))
            reach = 1
            while reach < planes:
                came = cyclic(carry, GROUP * reach)
                carry = jnp.where(self.plane >= reach, joined(came, carry), carry)
                reach *= 2
            self.other = carry

    def back(self):
        side = self.side
        if isinstance(self.other, list):
            carry = jnp.zeros_like(self.mine)
            for back, came in zip(range(len(self.other), 0, -1), self.other):
                carry = jnp.where(self.plane >= back, joined(carry, came), carry)
        else:
            carry = self.other
        carry = after(carry, self.mine)
        later = joined(carry, self.lower)
        self.mine = jnp.where(side == 0, carry, later)[:N]
        self.other = swapped(jnp.where(side == 0, later, carry)[:N], 2)

    def spread(self):
        core, side, mine, came = self.core, self.side, self.mine, self.other
        chip_in = jnp.concatenate(
            [jnp.where(side == 0, mine, came), jnp.where(side == 0, came, mine)], axis=1
        )
        next_in = jnp.exp(self.first[N : N + 1]) * chip_in + self.first[:N]
        self.mine = jnp.where(core == 0, chip_in, next_in)
        self.other = swapped(jnp.where(core == 0, next_in, chip_in), 1)

    def result(self):
        core, mine, came = self.core, self.mine, self.other
        return jnp.concatenate(
            [jnp.where(core == 0, mine, came), jnp.where(core == 0, came, mine)], axis=1
        )


def shards(queries, keys, values, x_in, log_decay, b_in, c_in, skip_d):
    device = lax.axis_index("ctx")
    core = device % 2
    side = (device // 2) % 2
    plane = device // GROUP
    flags = jnp.stack([core, side, jnp.where(plane > 0, 1, 0)], axis=0).astype(jnp.int32)
    groups = []
    for heads in CHUNKS:
        groups.append((sum(CHUNKS[: len(groups)]), heads))
    count = len(groups)
    own = [packed(*groups[0], keys, values)]
    for group in groups[1:]:
        own.append(packed(*group, after(keys, own[-1]), values))
    before = [cyclic(own[0], GROUP), cyclic(own[1], GROUP), cyclic(own[2], GROUP)]
    near_k, near_v = swapped(after(keys, own[1]), 1), swapped(after(values, own[1]), 1)
    skip_wide = jnp.repeat(skip_d, P_SIZE)[None, :]
    c_t = jnp.transpose(c_in)
    rest = (jnp.transpose(log_decay), jnp.transpose(b_in), c_t, skip_wide)
    part_a, state_a, cum = scan_local(0, after(x_in, own[1]), *rest)

    chosen, across, beside = {}, {}, {}

    def send(k, *others):
        came = after(before[k], *others)
        chosen[k] = jnp.where(side == 0, own[k], came)
        across[k] = swapped(chosen[k], 2)
        beside[k] = swapped(came, 1)
        if k + 3 < count:
            before.append(cyclic(after(own[k + 3], chosen[k]), GROUP))

    send(0, part_a)
    part_b, state_b, _ = scan_local(1, after(x_in, chosen[0]), *rest)
    carry = Carry(state_a, state_b, core, side, plane)
    send(1, part_b)
    out = None
    for k, (low, heads) in enumerate(groups):
        arrived = across[k]
        if k + 1 < count:
            arrived = after(arrived, chosen[k + 1])
        relayed = swapped(arrived, 1)
        if k == count - 1:
            scan_out = scan_finish(part_a, part_b, cum, c_t, after(carry.result(), out))
            relayed = after(relayed, scan_out)
        out = attend(
            flags, low, heads, queries, keys, values, before[k], arrived, beside[k],
            relayed, near_k, near_v, () if k == 0 else (out,),
        )
        if k + 2 < count:
            send(k + 2, out)
        if k in STEPS:
            carry.advance(out)
    return (out, scan_out)


def solution(mesh):
    row = P(("seqs", "ctx"), None)
    in_specs = (row,) * 7 + (P(),)
    return jax.shard_map(
        shards, mesh=mesh, in_specs=in_specs, out_specs=(row, row), check_vma=False
    )
```

```python
import functools

import jax
import jax.numpy as jnp
from jax import lax
from jax.experimental import pallas as pl
from jax.experimental.pallas import tpu as pltpu
from jax.sharding import PartitionSpec as P

TOK_DEV = 512
WINDOW = 2048
AH = 16
HD = 128
SCAN_HEADS = 32
P_SIZE = 64
N = 64
GROUP = WINDOW // TOK_DEV
SUB = 128
CHUNKS = (4, 4, 3, 3, 2)
STEPS = (0, 1, 2, 3)
NEG = -1e30
EXP_SCALE = HD ** (-0.5) * 1.4426950408889634
F32 = jnp.float32
BF16 = jnp.bfloat16


def in_hbm(*arrays):
    return [pltpu.with_memory_space_constraint(array, pltpu.HBM) for array in arrays]


def cyclic(array, by):
    count = lax.axis_size("ctx")
    return lax.ppermute(array, "ctx", [(i, (i + by) % count) for i in range(count)])


def swapped(array, bit):
    count = lax.axis_size("ctx")
    return lax.ppermute(array, "ctx", [(i, i ^ bit) for i in range(count)])


def dot_t(a, b):
    return lax.dot_general(a, b, (((1,), (1,)), ((), ())), preferred_element_type=F32)


def dot_v(a, b):
    return lax.dot_general(a, b, (((0,), (0,)), ((), ())), preferred_element_type=F32)


def dot_f32(a, b):
    return jnp.dot(a, b, preferred_element_type=F32)


def attend_kernel(flags, q, k, v, z, d, e, g, xk, xv, *rest):
    out, near = rest[-2:]
    odd, later, full = flags[0], flags[1], flags[2]
    half = TOK_DEV // 2

    @pl.when(odd == 1)
    def _():
        near[0] = xk[...]
        near[1] = xv[...]

    @pl.when(odd == 0)
    def _():
        near[...] = e[...]

    def body(masked):
        q_all = q[...]
        q_lo, q_hi = q[:half, :], q[half:, :]
        key = lax.broadcasted_iota(jnp.int32, (half, half), 0)
        query = lax.broadcasted_iota(jnp.int32, (half, half), 1)
        causal = key <= query
        k_lo, k_hi = k[:half, :], k[half:, :]
        z_lo, z_hi = z[0, :half, :], z[0, half:, :]
        before_lo, before_hi = dot_t(z_lo, q_lo), dot_t(z_hi, q_hi)
        s10 = dot_t(z_hi, q_lo)
        s2, s3, s4 = dot_t(d[0], q_all), dot_t(near[0], q_all), dot_t(g[0], q_all)
        if masked:
            before_lo, before_hi = jnp.full_like(before_lo, NEG), jnp.full_like(before_hi, NEG)
            s10 = jnp.full_like(s10, NEG)
            bias_d = jnp.where(later == 1, 0.0, NEG)
            bias_e = jnp.where(odd == 1, 0.0, NEG)
            s2, s3, s4 = s2 + bias_d, s3 + bias_e, s4 + bias_d
        s00 = jnp.where(causal, dot_t(k_lo, q_lo), before_lo)
        s01 = dot_t(k_lo, q_hi)
        s11 = jnp.where(causal, dot_t(k_hi, q_hi), before_hi)
        most = lambda s: jnp.max(s, axis=0, keepdims=True)
        tri = jnp.concatenate(
            [jnp.maximum(most(s00), most(s10)), jnp.maximum(most(s01), most(s11))], axis=1
        )
        top = jnp.maximum(jnp.maximum(tri, most(s2)), jnp.maximum(most(s3), most(s4)))
        top = top * EXP_SCALE
        t_lo, t_hi = top[:, :half], top[:, half:]
        p00, p10 = jnp.exp2(s00 * EXP_SCALE - t_lo), jnp.exp2(s10 * EXP_SCALE - t_lo)
        p01, p11 = jnp.exp2(s01 * EXP_SCALE - t_hi), jnp.exp2(s11 * EXP_SCALE - t_hi)
        add = lambda p: jnp.sum(p, axis=0, keepdims=True)
        total = jnp.concatenate([add(p00) + add(p10), add(p01) + add(p11)], axis=1)
        mine = lambda p: jnp.where(causal, p, 0.0).astype(BF16)
        theirs = lambda p: jnp.where(causal, 0.0, p).astype(BF16)
        v_lo, v_hi = v[:half, :], v[half:, :]
        w_lo, w_hi = z[1, :half, :], z[1, half:, :]
        acc_lo = dot_v(v_lo, mine(p00)) + dot_v(w_lo, theirs(p00)) + dot_v(w_hi, p10.astype(BF16))
        acc_hi = dot_v(v_hi, mine(p11)) + dot_v(w_hi, theirs(p11)) + dot_v(v_lo, p01.astype(BF16))
        acc = jnp.concatenate([acc_lo, acc_hi], axis=1)
        for s, block in ((s2, d), (s3, near), (s4, g)):
            prob = jnp.exp2(s * EXP_SCALE - top)
            total = total + add(prob)
            acc = acc + dot_v(block[1], prob.astype(BF16))
        out[...] = jnp.transpose(acc / total).astype(BF16)

    @pl.when(full == 1)
    def _():
        body(False)

    @pl.when(full == 0)
    def _():
        body(True)


def attend(flags, low, heads, queries, keys, values, z, d, e, g, xk, xv, sofar):
    wide = pl.BlockSpec((TOK_DEV, HD), lambda j, f: (0, low + j))
    pair = pl.BlockSpec((2, TOK_DEV, HD), lambda j, f: (0, 0, j))
    left = pl.BlockSpec(memory_space=pl.ANY)
    return pl.pallas_call(
        attend_kernel,
        name="attend",
        out_shape=jax.ShapeDtypeStruct((TOK_DEV, AH * HD), BF16),
        grid_spec=pltpu.PrefetchScalarGridSpec(
            num_scalar_prefetch=1,
            grid=(heads,),
            in_specs=[wide, wide, wide, pair, pair, pair, pair, wide, wide] + [left] * len(sofar),
            out_specs=wide,
            scratch_shapes=[pltpu.VMEM((2, TOK_DEV, HD), BF16)],
        ),
        input_output_aliases={10: 0} if sofar else {},
        compiler_params=pltpu.CompilerParams(vmem_limit_bytes=32 << 20),
    )(flags, *in_hbm(queries, keys, values), z, d, e, g, *in_hbm(xk, xv), *sofar)


def packed(low, heads, keys, values):
    cols = slice(low * HD, (low + heads) * HD)
    return jnp.stack([keys[:, cols], values[:, cols]])


def split3(a):
    hi = a.astype(BF16)
    rest = a - hi.astype(F32)
    mid = rest.astype(BF16)
    low = (rest - mid.astype(F32)).astype(BF16)
    return hi, mid, low


def split2(a):
    hi = a.astype(BF16)
    return hi, (a - hi.astype(F32)).astype(BF16)


def pick(head, width):
    row = lax.broadcasted_iota(jnp.int32, (3 * SCAN_HEADS, width), 0) % SCAN_HEADS
    return (row == head).astype(BF16)


PAIRS = 2


def local_kernel(base, x, decay_t, b_t, c_t, skip, part, state, cum_out, cums, cum_t, cross, b, c):
    step = pl.program_id(0)
    lane = lax.broadcasted_iota(jnp.int32, (SUB, SUB), 1)
    lower = lax.broadcasted_iota(jnp.int32, (SUB, SUB), 0) >= lane
    left = lane < P_SIZE

    @pl.when(step == 0)
    def _():
        t = lax.broadcasted_iota(jnp.int32, (TOK_DEV, TOK_DEV), 0)
        u = lax.broadcasted_iota(jnp.int32, (TOK_DEV, TOK_DEV), 1)
        until = (t <= u).astype(BF16)
        hi, mid, low = split3(decay_t[...])
        total = dot_f32(hi, until) + dot_f32(mid, until) + dot_f32(low, until)
        cum_t[...] = total
        total = jnp.transpose(total)
        cum_out[...] = total
        hi, mid, low = split3(total)
        cums[:, 0:32] = hi
        cums[:, 32:64] = mid
        cums[:, 64:96] = low
        b[...] = jnp.transpose(b_t[...].astype(F32)).astype(BF16)
        c[...] = jnp.transpose(c_t[...].astype(F32)).astype(BF16)
        for s in range(TOK_DEV // SUB):
            at = pl.ds(s * SUB, SUB)
            cross[at, :] = jnp.where(lower, dot_t(c[at, :], b[at, :]), 0.0)

    for pair in range(PAIRS):
        first = 2 * (step * PAIRS + pair) + base
        cols = slice(pair * SUB, (pair + 1) * SUB)
        cum_a = dot_f32(cums[...], pick(first, SUB))
        cum_b = dot_f32(cums[...], pick(first + 1, SUB))
        row_a = cum_t[pl.ds(first, 1), :]
        row_b = cum_t[pl.ds(first + 1, 1), :]
        carry = jnp.zeros((N, SUB), F32)
        before = jnp.zeros((1, SUB), F32)
        for s in range(TOK_DEV // SUB):
            at = slice(s * SUB, (s + 1) * SUB)
            col_a, col_b = cum_a[at, :], cum_b[at, :]
            both = jnp.where(left, col_a, col_b)
            xf = x[at, cols].astype(F32)
            inner = cross[at, :]
            gap_a = jnp.minimum(col_a - row_a[:, at], 0.0)
            gap_b = jnp.minimum(col_b - row_b[:, at], 0.0)
            mix_a = (jnp.exp(gap_a) * inner).astype(BF16)
            mix_b = (jnp.exp(gap_b) * inner).astype(BF16)
            x_a = jnp.where(left, xf, 0.0).astype(BF16)
            x_b = jnp.where(left, 0.0, xf).astype(BF16)
            y = dot_f32(
                jnp.concatenate([mix_a, mix_b], axis=1), jnp.concatenate([x_a, x_b], axis=0)
            )
            if s > 0:
                hi, low = split2(carry)
                cs = c[at, :]
                reach = dot_f32(
                    jnp.concatenate([cs, cs], axis=1), jnp.concatenate([hi, low], axis=0)
                )
                y = y + jnp.exp(both - before) * reach
            part[at, cols] = y + skip[:, cols] * xf
            end = both[SUB - 1 : SUB, :]
            weighted = (xf * jnp.exp(end - both)).astype(BF16)
            added = dot_f32(b_t[:, at], weighted)
            carry = jnp.exp(end - before) * carry + added
            before = end
        state[0:N, cols] = carry
        state[N : N + 8, cols] = jnp.broadcast_to(before, (8, SUB))


def scan_local(half, x_in, decay_t, b_t, c_t, skip_wide):
    width = PAIRS * SUB
    lanes = SCAN_HEADS * P_SIZE // 2
    steps = lanes // width
    whole = lambda shape: pl.BlockSpec(shape, lambda j: (0, 0))
    return pl.pallas_call(
        functools.partial(local_kernel, half * SCAN_HEADS // 2),
        name="scan_local",
        out_shape=(
            jax.ShapeDtypeStruct((TOK_DEV, lanes), F32),
            jax.ShapeDtypeStruct((N + 8, lanes), F32),
            jax.ShapeDtypeStruct((TOK_DEV, SCAN_HEADS), F32),
        ),
        grid=(steps,),
        in_specs=[
            pl.BlockSpec((TOK_DEV, width), lambda j: (0, half * steps + j)),
            whole((SCAN_HEADS, TOK_DEV)),
            whole((N, TOK_DEV)),
            whole((N, TOK_DEV)),
            pl.BlockSpec((1, width), lambda j: (0, half * steps + j)),
        ],
        out_specs=(
            pl.BlockSpec((TOK_DEV, width), lambda j: (0, j)),
            pl.BlockSpec((N + 8, width), lambda j: (0, j)),
            whole((TOK_DEV, SCAN_HEADS)),
        ),
        scratch_shapes=[
            pltpu.VMEM((TOK_DEV, 3 * SCAN_HEADS), BF16),
            pltpu.VMEM((SCAN_HEADS, TOK_DEV), F32),
            pltpu.VMEM((TOK_DEV, SUB), F32),
            pltpu.VMEM((TOK_DEV, N), BF16),
            pltpu.VMEM((TOK_DEV, N), BF16),
        ],
        compiler_params=pltpu.CompilerParams(vmem_limit_bytes=32 << 20),
    )(*in_hbm(x_in), decay_t, b_t, c_t, skip_wide)


def finish_kernel(part_a, part_b, cum, c_t, carried, out):
    step = pl.program_id(0)
    part = jnp.where(step < 2, part_a[...], part_b[...])
    width = out.shape[1]
    hi, mid, low = split3(cum[...])
    row = lax.broadcasted_iota(jnp.int32, (3 * SCAN_HEADS, width), 0) % SCAN_HEADS
    lane = lax.broadcasted_iota(jnp.int32, (3 * SCAN_HEADS, width), 1) // P_SIZE
    chosen = (row == lane + step * (width // P_SIZE)).astype(BF16)
    wide = dot_f32(jnp.concatenate([hi, mid, low], axis=1), chosen)
    hi, low = split2(carried[...])
    cs = c_t[...]
    reach = dot_v(jnp.concatenate([cs, cs], axis=0), jnp.concatenate([hi, low], axis=0))
    out[...] = (part + jnp.exp(wide) * reach).astype(BF16)


def scan_finish(part_a, part_b, cum, c_t, carried):
    width = 512
    whole = lambda shape: pl.BlockSpec(shape, lambda j: (0, 0))
    column = lambda rows: pl.BlockSpec((rows, width), lambda j: (0, j))
    return pl.pallas_call(
        finish_kernel,
        name="scan_finish",
        out_shape=jax.ShapeDtypeStruct((TOK_DEV, SCAN_HEADS * P_SIZE), BF16),
        grid=(SCAN_HEADS * P_SIZE // width,),
        in_specs=[
            pl.BlockSpec((TOK_DEV, width), lambda j: (0, jnp.minimum(j, 1))),
            pl.BlockSpec((TOK_DEV, width), lambda j: (0, jnp.maximum(j - 2, 0))),
            whole((TOK_DEV, SCAN_HEADS)),
            whole((N, TOK_DEV)),
            column(N),
        ],
        out_specs=column(TOK_DEV),
        compiler_params=pltpu.CompilerParams(vmem_limit_bytes=32 << 20),
    )(part_a, part_b, cum, c_t, carried)


def joined(earlier, following):
    total = earlier[N:] + following[N:]
    state = jnp.exp(following[N : N + 1]) * earlier[:N] + following[:N]
    return jnp.concatenate([state, total], axis=0)


def after(value, *others):
    return lax.optimization_barrier((value,) + others)[0]


class Carry:
    def __init__(self, state_a, state_b, core, side, plane):
        self.core, self.side, self.plane = core, side, plane
        self.mine = jnp.where(core == 0, state_a, state_b)
        self.other = swapped(jnp.where(core == 0, state_b, state_a), 1)
        self.steps = [self.chip, self.across, self.back, self.spread]

    def advance(self, *others):
        if self.steps:
            self.mine = after(self.mine, *others)
            self.other = after(self.other, *others)
            self.steps.pop(0)()

    def chip(self):
        core, side, quarter = self.core, self.side, self.mine.shape[1] // 2
        self.first = jnp.where(core == 0, self.mine, self.other)
        second = jnp.where(core == 0, self.other, self.mine)
        chip = joined(self.first, second)
        self.mine = jnp.where(side == 0, chip[:, :quarter], chip[:, quarter:])
        self.other = swapped(jnp.where(side == 0, chip[:, quarter:], chip[:, :quarter]), 2)

    def across(self):
        self.lower = jnp.where(self.side == 0, self.mine, self.other)
        upper = jnp.where(self.side == 0, self.other, self.mine)
        total = joined(self.lower, upper)
        planes = lax.axis_size("ctx") // GROUP
        self.mine = total
        if planes <= 4:
            self.other = [cyclic(total, GROUP * back) for back in range(planes - 1, 0, -1)]
        else:
            carry = jnp.where(self.plane >= 1, cyclic(total, GROUP), jnp.zeros_like(total))
            reach = 1
            while reach < planes:
                came = cyclic(carry, GROUP * reach)
                carry = jnp.where(self.plane >= reach, joined(came, carry), carry)
                reach *= 2
            self.other = carry

    def back(self):
        side = self.side
        if isinstance(self.other, list):
            carry = jnp.zeros_like(self.mine)
            for back, came in zip(range(len(self.other), 0, -1), self.other):
                carry = jnp.where(self.plane >= back, joined(carry, came), carry)
        else:
            carry = self.other
        carry = after(carry, self.mine)
        later = joined(carry, self.lower)
        self.mine = jnp.where(side == 0, carry, later)[:N]
        self.other = swapped(jnp.where(side == 0, later, carry)[:N], 2)

    def spread(self):
        core, side, mine, came = self.core, self.side, self.mine, self.other
        chip_in = jnp.concatenate(
            [jnp.where(side == 0, mine, came), jnp.where(side == 0, came, mine)], axis=1
        )
        next_in = jnp.exp(self.first[N : N + 1]) * chip_in + self.first[:N]
        self.mine = jnp.where(core == 0, chip_in, next_in)
        self.other = swapped(jnp.where(core == 0, next_in, chip_in), 1)

    def result(self):
        core, mine, came = self.core, self.mine, self.other
        return jnp.concatenate(
            [jnp.where(core == 0, mine, came), jnp.where(core == 0, came, mine)], axis=1
        )


def shards(queries, keys, values, x_in, log_decay, b_in, c_in, skip_d):
    device = lax.axis_index("ctx")
    core = device % 2
    side = (device // 2) % 2
    plane = device // GROUP
    flags = jnp.stack([core, side, jnp.where(plane > 0, 1, 0)], axis=0).astype(jnp.int32)
    groups = []
    for heads in CHUNKS:
        groups.append((sum(CHUNKS[: len(groups)]), heads))
    count = len(groups)
    own = [packed(*groups[0], keys, values)]
    for group in groups[1:]:
        own.append(packed(*group, after(keys, own[-1]), values))
    before = [cyclic(own[0], GROUP), cyclic(own[1], GROUP), cyclic(own[2], GROUP)]
    near_k, near_v = swapped(after(keys, own[1]), 1), swapped(after(values, own[1]), 1)
    skip_wide = jnp.repeat(skip_d, P_SIZE)[None, :]
    c_t = jnp.transpose(c_in)
    rest = (jnp.transpose(log_decay), jnp.transpose(b_in), c_t, skip_wide)
    part_a, state_a, cum = scan_local(0, after(x_in, own[1]), *rest)

    chosen, across, beside = {}, {}, {}

    def send(k, *others):
        came = after(before[k], *others)
        chosen[k] = jnp.where(side == 0, own[k], came)
        across[k] = swapped(chosen[k], 2)
        beside[k] = swapped(came, 1)
        if k + 3 < count:
            before.append(cyclic(after(own[k + 3], chosen[k]), GROUP))

    send(0, part_a)
    part_b, state_b, _ = scan_local(1, after(x_in, chosen[0]), *rest)
    carry = Carry(state_a, state_b, core, side, plane)
    send(1, part_b)
    out = None
    for k, (low, heads) in enumerate(groups):
        arrived = across[k]
        if k + 1 < count:
            arrived = after(arrived, chosen[k + 1])
        relayed = swapped(arrived, 1)
        if k == count - 1:
            scan_out = scan_finish(part_a, part_b, cum, c_t, after(carry.result(), out))
            relayed = after(relayed, scan_out)
        out = attend(
            flags, low, heads, queries, keys, values, before[k], arrived, beside[k],
            relayed, near_k, near_v, () if k == 0 else (out,),
        )
        if k + 2 < count:
            send(k + 2, out)
        if k in STEPS:
            carry.advance(out)
    return (out, scan_out)


def solution(mesh):
    row = P(("seqs", "ctx"), None)
    in_specs = (row,) * 7 + (P(),)
    return jax.shard_map(
        shards, mesh=mesh, in_specs=in_specs, out_specs=(row, row), check_vma=False
    )
```
